32 devices in a mesh: req: 2 (over x), ctx: 4 (over y, core), tp: 4 (over z).
Axes of the slice: x: 2, y: 2, z: 4, core: 2. Of those that a mesh axis runs over, the one named last changes fastest.
Arguments:
- queries: bfloat16 [512, 16, 128], P('req', 'tp'), may hold values from -5 to 5
- new_keys: bfloat16 [512, 4, 128], P('req', 'tp'), may hold values from -5 to 5
- new_values: bfloat16 [512, 4, 128], P('req', 'tp'), may hold values from -24 to 24
- cache_keys: bfloat16 [2, 8192, 4, 128], P('req', 'ctx', 'tp'), may hold values from -5 to 5
- cache_values: bfloat16 [2, 8192, 4, 128], P('req', 'ctx', 'tp'), may hold values from -24 to 24
- cache_lengths: int32 [2], replicated, may hold values from 1 to 8192, as said below
- residual: bfloat16 [512, 2048], P(('req', 'ctx'), 'tp'), may hold values from -24 to 24
- out_weight: bfloat16 [2048, 2048], P('tp', 'ctx'), may hold values from -0.52734375 to 0.52734375
- norm_gain: float32 [2048], replicated, may hold values from 0.1 to 1.9
- expert_ids: int32 [512, 6], P(('req', 'ctx')), may hold values from 0 to 63, all different within a row; in each aligned block of 64 rows (0 to 63, 64 to 127, ...) at most 8 rows name the same one
- gate_weights: float32 [512, 6], P(('req', 'ctx')), may hold values from 0.1 to 1
- w_gate: bfloat16 [64, 2048, 1408], P('req', 'ctx', 'tp'), may hold values from -0.125 to 0.125
- w_up: bfloat16 [64, 2048, 1408], P('req', 'ctx', 'tp'), may hold values from -0.125 to 0.125
- w_down: bfloat16 [64, 1408, 2048], P('req', 'tp', 'ctx'), may hold values from -0.15625 to 0.15625
Outputs:
- layer_out: bfloat16 [512, 2048], P(('req', 'ctx'), 'tp')
The draws below stay inside these ranges and needn't reach their ends.
Inputs may be any that keep to these rules, and one draw needn't show every extreme that they name: `cache_lengths`: the longest cached length equals 8192. `expert_ids`: within each aligned block of 64 tokens no expert is named by more than 8 routes, a bound that some block reaches.
All inputs are finite; a program needn't handle non-finite values.
Results may differ from the reference program's by a relative error of at most 0.006.
Values may be sent and summed in bfloat16 or wider, within the bound.
A program may use at most 384 MiB of HBM per device.

```python
import math
import jax
import jax.numpy as jnp
import numpy as np
from jax import lax

D = 2048
H = 16
KVH = 4
HD = 128
FF = 1408
EXPERTS = 64
TOP = 6
TOK_DEV = 256
CTX_DEV = 2048
CAP = 8
REQS = 2
TOKENS = 512
CACHE = 8192
FF_DEV = 352
MOE_DEV = 64
N_CTX = 4
N_TP = 4


def draw_queries(key, part):
    noise_key = jax.random.fold_in(key, 1)
    base = jax.random.truncated_normal(noise_key, -4.0, 4.0, (TOKENS, H, HD), jnp.float32)
    return base.astype(jnp.bfloat16)


def draw_new_keys(key, part):
    noise_key = jax.random.fold_in(key, 2)
    base = jax.random.truncated_normal(noise_key, -4.0, 4.0, (TOKENS, KVH, HD), jnp.float32)
    return base.astype(jnp.bfloat16)


def draw_cache_keys(key, part):
    noise_key = jax.random.fold_in(key, 3)
    base = jax.random.truncated_normal(noise_key, -4.0, 4.0, (REQS, CACHE, KVH, HD), jnp.float32)
    return base.astype(jnp.bfloat16)


def draw_cache_lengths(key, part):
    others = jax.random.randint(jax.random.fold_in(key, 11), (REQS,), 1, CACHE, jnp.int32)
    longest = jax.random.randint(jax.random.fold_in(key, 12), (), 0, REQS, jnp.int32)
    chosen = jnp.arange(REQS, dtype=jnp.int32) == longest
    return jnp.where(chosen, jnp.int32(CACHE), others).astype(jnp.int32)


def draw_residual(key, part):
    row_scale = jnp.exp(jax.random.uniform(jax.random.fold_in(key, 4), (TOKENS, 1), jnp.float32, jnp.log(0.3), jnp.log(3.0)))
    column_scale = jnp.exp(jax.random.uniform(jax.random.fold_in(key, 5), (1, D), jnp.float32, jnp.log(0.5), jnp.log(2.0)))
    base = jax.random.truncated_normal(jax.random.fold_in(key, 8), -4.0, 4.0, (TOKENS, D), jnp.float32)
    return (base * row_scale * column_scale).astype(jnp.bfloat16)


def steps_of(key, shape, cuts, smallest, top_value):
    def one(axis_at, shards_of):
        draws = jax.random.uniform(jax.random.fold_in(jax.random.fold_in(key, 6), axis_at), (shards_of,), jnp.float32, smallest / len(cuts), top_value / len(cuts))
        return jnp.repeat(jnp.exp(draws), shape[axis_at] // shards_of).reshape((-1,) + (1,) * (len(shape) - axis_at - 1))

    loudness = one(*cuts[0])
    for cut in cuts[1:]:
        loudness = loudness * one(*cut)
    return loudness


def deal_out(own_key, own, number, rows, amount, top, reach, slope):
    ranking = jax.random.permutation(own_key, amount)
    crowded, ordinary = shares(amount, rows * top, reach, slope, True), shares(amount, rows * top, reach, slope, False)
    places = jnp.arange(amount)

    def named(lengths, rotation):
        used = int((lengths > 0).sum())
        fixed = max(1, used // 4)
        moved = fixed + (places - fixed + rotation * (used - fixed)) % max(1, amount - fixed)
        return jnp.zeros((amount,), jnp.int32).at[ranking[jnp.where(places < fixed, places, moved)]].set(jnp.asarray(lengths, jnp.int32))

    lengths = jnp.where(number % 4 == 0, named(crowded, number // 4), named(ordinary, number - number // 4 - 1))
    mixed = jax.random.permutation(jax.random.fold_in(own, 3), amount)
    donor, receiver = mixed[0:amount // 2 * 2:2], mixed[1:amount // 2 * 2:2]
    room = jnp.minimum(lengths[donor] - 1, reach - lengths[receiver]) // 2
    room = jnp.where((donor == ranking[0]) | (receiver == ranking[0]) | (lengths[receiver] == 0), 0, jnp.maximum(room, 0))
    moved = jax.random.randint(jax.random.fold_in(own, 4), (amount // 2,), 0, 1 << 20) % (room + 1)
    lengths = lengths.at[donor].add(-moved).at[receiver].add(moved)
    items = jnp.searchsorted(jnp.cumsum(lengths), jnp.arange(rows * top), side="right").astype(jnp.int32)
    grid = items.reshape(top, rows).T
    grid = grid[jax.random.permutation(jax.random.fold_in(own, 1), rows)]
    rotation = jax.random.randint(jax.random.fold_in(own, 2), (rows, 1), 0, top)
    return jnp.take_along_axis(grid, (jnp.arange(top)[None, :] + rotation) % top, axis=1)


def shares(amount, total, limit, lean, full):
    loads = [(1 << 20) // math.isqrt(grade ** lean) + 1 for grade in range(1, amount + 1)]
    largest = limit if full else min(limit, max(-(-total // amount), total * loads[0] // sum(loads)))
    least = 1 if total - largest >= amount - 1 else 0
    given, rest = [largest] + [least] * (amount - 1), total - largest - least * (amount - 1)
    while rest > 0:
        free = [i for i in range(1, amount) if given[i] < largest] or [i for i in range(1, amount) if given[i] < limit]
        pool, left = sum([loads[i] for i in free]), rest
        for i in free:
            more = min(limit - given[i], max(1, left * loads[i] // pool), rest)
            given[i] = given[i] + more
            rest = rest - more
    return np.array(given)


def scatter_about(stream_key, shape, spread, most, split=(), held_as=jnp.bfloat16):
    factor_of = steps_of(stream_key, shape, split, -0.22, 0.18) if split else 1.0
    drawn = jax.random.normal(stream_key, shape, jnp.float32) * spread * factor_of
    return jnp.minimum(jnp.maximum(drawn, -most), most).astype(held_as)


def setup_inputs(seed: int = 0) -> dict:
    arg_keys = jax.random.split(jax.random.key(seed), 15)
    queries = draw_queries(jax.random.fold_in(arg_keys[14], 71), 0)
    new_keys = draw_new_keys(jax.random.fold_in(arg_keys[14], 71), 0)
    new_values = scatter_about(arg_keys[2], (TOKENS, KVH, HD), 4.0, 24.0, ((0, 2), (1, 4)))
    cache_keys = draw_cache_keys(jax.random.fold_in(arg_keys[14], 71), 0)
    cache_values = scatter_about(arg_keys[4], (REQS, CACHE, KVH, HD), 4.0, 24.0, ((0, 2), (1, 4), (2, 4)))
    cache_lengths = draw_cache_lengths(jax.random.fold_in(arg_keys[14], 71), 0)
    residual = draw_residual(jax.random.fold_in(arg_keys[14], 71), 0)
    out_weight = scatter_about(arg_keys[7], (H * HD, D), (4.0 / (H * HD) ** 0.5), 0.52734375, ((0, 4), (1, 4)))
    norm_gain = jnp.clip(1.0 + 0.18 * jax.random.normal(arg_keys[8], (D,), jnp.float32), 0.1, 1.9)
    expert_ids_keys = jax.random.split(jax.random.fold_in(arg_keys[9], 1), TOKENS // MOE_DEV)
    expert_ids_turns = jax.random.permutation(jax.random.fold_in(arg_keys[9], 3), TOKENS // MOE_DEV)
    expert_ids = jax.vmap(lambda own, number: deal_out(jax.random.fold_in(arg_keys[9], 2), own, number, MOE_DEV, EXPERTS, TOP, CAP, 2))(expert_ids_keys, expert_ids_turns).reshape((TOKENS, TOP))
    gate_weights = jnp.clip(0.1 + 0.9 * jax.random.uniform(arg_keys[10], (TOKENS, TOP), jnp.float32) ** steps_of(arg_keys[10], (TOKENS, TOP), ((0, 8),), -0.2, 0.2), 0.1, 1.0)
    w_gate = scatter_about(arg_keys[11], (EXPERTS, D, FF), D ** -0.5, 0.125, ((0, 2), (1, 4), (2, 4)))
    w_up = scatter_about(arg_keys[12], (EXPERTS, D, FF), D ** -0.5, 0.125, ((0, 2), (1, 4), (2, 4)))
    w_down = scatter_about(arg_keys[13], (EXPERTS, FF, D), FF ** -0.5, 0.15625, ((0, 2), (1, 4), (2, 4)))
    return {"queries": queries, "new_keys": new_keys, "new_values": new_values, "cache_keys": cache_keys, "cache_values": cache_values, "cache_lengths": cache_lengths, "residual": residual, "out_weight": out_weight, "norm_gain": norm_gain, "expert_ids": expert_ids, "gate_weights": gate_weights, "w_gate": w_gate, "w_up": w_up, "w_down": w_down}


masked_score = -1e+30

def attend_request(request, queries, new_keys, new_values, cache_keys, cache_values, cache_lengths):
    scale = 1.0 / HD ** 0.5
    start = request * TOK_DEV
    query_rows = lax.dynamic_slice_in_dim(queries, start, TOK_DEV, 0)
    fresh_keys = lax.dynamic_slice_in_dim(new_keys, start, TOK_DEV, 0)
    fresh_values = lax.dynamic_slice_in_dim(new_values, start, TOK_DEV, 0)
    old_keys = lax.dynamic_index_in_dim(cache_keys, request, 0, keepdims=False)
    old_values = lax.dynamic_index_in_dim(cache_values, request, 0, keepdims=False)
    length = lax.dynamic_index_in_dim(cache_lengths, request, 0, keepdims=False)
    key_rows = jnp.concatenate([old_keys, fresh_keys], 0)
    cache_valid = (jnp.arange(CACHE, dtype=jnp.int32) < length).reshape(N_CTX, CTX_DEV)
    positions = jnp.arange(TOK_DEV, dtype=jnp.int32)
    causal = positions[None, :] <= positions[:, None]
    group_size = H // KVH
    pieces = []
    for group in range(KVH):
        grouped = query_rows[:, group * group_size:(group + 1) * group_size, :].reshape(TOK_DEV * group_size, HD)
        scores = jnp.dot(grouped, key_rows[:, group, :].T, preferred_element_type=jnp.float32) * scale
        scores = scores.reshape(TOK_DEV, group_size, CACHE + TOK_DEV)
        cached = scores[:, :, :CACHE].reshape(TOK_DEV, group_size, N_CTX, CTX_DEV)
        cached = jnp.where(cache_valid[None, None], cached, masked_score)
        fresh = jnp.where(causal[:, None, :], scores[:, :, CACHE:], masked_score)
        cached_max = lax.optimization_barrier(jnp.max(cached, -1))
        last_max = jnp.maximum(cached_max[:, :, -1], lax.optimization_barrier(jnp.max(fresh, -1)))
        block_max = jnp.concatenate([cached_max[:, :, :-1], last_max[:, :, None]], -1)
        cached_weights = jnp.where(cache_valid[None, None], jnp.exp(cached - block_max[..., None]), 0.0)
        fresh_weights = jnp.where(causal[:, None, :], jnp.exp(fresh - last_max[..., None]), 0.0)
        block_total = lax.optimization_barrier(jnp.sum(cached_weights, -1))
        block_total = block_total.at[:, :, -1].add(lax.optimization_barrier(jnp.sum(fresh_weights, -1)))
        cached_rounded_scores = lax.optimization_barrier(cached_weights.astype(jnp.bfloat16)).astype(jnp.float32)
        fresh_round = lax.optimization_barrier(fresh_weights.astype(jnp.bfloat16)).astype(jnp.float32)
        block_value_rows = old_values[:, group, :].reshape(N_CTX, CTX_DEV, HD).astype(jnp.float32)
        block_partial_sum = jnp.einsum('osqz,qzl->osql', cached_rounded_scores, block_value_rows, precision=lax.Precision.HIGHEST)
        fresh_sum = jnp.einsum('tgk,kd->tgd', fresh_round, fresh_values[:, group, :].astype(jnp.float32), precision=lax.Precision.HIGHEST)
        block_partial_sum = block_partial_sum.at[:, :, -1].add(fresh_sum)
        top = lax.optimization_barrier(jnp.max(block_max, -1, keepdims=True))
        factor = jnp.exp(block_max - top)
        total = lax.optimization_barrier(jnp.sum(factor * block_total, -1))
        weighted = lax.optimization_barrier(jnp.sum(factor[..., None] * block_partial_sum, 2))
        pieces.append(weighted / total[..., None])
    return jnp.concatenate(pieces, 1).reshape(TOK_DEV, H * HD).astype(jnp.bfloat16)

def reference(queries, new_keys, new_values, cache_keys, cache_values, cache_lengths, residual, out_weight, norm_gain, expert_ids, gate_weights, w_gate, w_up, w_down):

    def one_request(request):
        return attend_request(request, queries, new_keys, new_values, cache_keys, cache_values, cache_lengths)
    attention_result = lax.map(one_request, jnp.arange(REQS, dtype=jnp.int32)).reshape(TOKENS, H * HD)
    hidden = residual.astype(jnp.float32) + jnp.dot(attention_result, out_weight, preferred_element_type=jnp.float32)
    mean_square = lax.optimization_barrier(jnp.mean(hidden * hidden, -1, keepdims=True))
    normed = (hidden * lax.rsqrt(mean_square + 1e-06) * norm_gain).astype(jnp.bfloat16)
    flat_ids = expert_ids.reshape(-1)
    flat_gates = gate_weights.reshape(-1)
    flat_tokens = (jnp.arange(TOKENS * TOP, dtype=jnp.int32) // TOP).astype(jnp.int32)
    slot_limit = CAP * (TOKENS // MOE_DEV)

    def expert_step(accum_sum, expert):
        matches = flat_ids == expert
        count = jnp.sum(matches.astype(jnp.int32))
        picked_rows = jnp.nonzero(matches, size=slot_limit, fill_value=0)[0].astype(jnp.int32)
        is_live = jnp.arange(slot_limit, dtype=jnp.int32) < count
        token_ids = flat_tokens[picked_rows]
        factors = jnp.where(is_live, flat_gates[picked_rows], 0.0)
        gathered = normed[token_ids]
        gate_act = jnp.dot(gathered, w_gate[expert], preferred_element_type=jnp.float32)
        up_act = jnp.dot(gathered, w_up[expert], preferred_element_type=jnp.float32)
        inner = (jax.nn.silu(gate_act) * up_act).astype(jnp.bfloat16)
        down_rows = w_down[expert]
        routed_tokens = jnp.zeros((slot_limit, D), jnp.float32)
        for group in range(N_TP):
            piece_out = jnp.dot(inner[:, group * FF_DEV:(group + 1) * FF_DEV], down_rows[group * FF_DEV:(group + 1) * FF_DEV, :], preferred_element_type=jnp.float32)
            routed_tokens = routed_tokens + piece_out.astype(jnp.bfloat16).astype(jnp.float32)
        accum_sum = accum_sum.at[token_ids].add(factors[:, None] * routed_tokens)
        return (accum_sum, None)
    expert_mixture, unused = lax.scan(expert_step, jnp.zeros((TOKENS, D), jnp.float32), jnp.arange(EXPERTS, dtype=jnp.int32))
    return (hidden + expert_mixture).astype(jnp.bfloat16)
```

```python
import functools
import jax
import jax.numpy as jnp
from jax import lax
from jax.experimental import pallas as pl
from jax.experimental.pallas import tpu as pltpu
from jax.sharding import PartitionSpec as P

TOP = 6
CAP = 8
MASKED = -1e30
F32 = jnp.float32
BF16 = jnp.bfloat16
CHUNKS = 4
PIECES = 2
FUSED_BYTES = 4 * 1024 * 1024


def dot(a, b, contract, kind=F32):
    return lax.dot_general(a, b, (contract, ((), ())), preferred_element_type=kind)


def layer_kernel(
    dims,
    len_ref,
    ids_ref,
    gw_ref,
    gain_ref,
    res_ref,
    q_hbm,
    ck_hbm,
    cv_hbm,
    nk_hbm,
    nv_hbm,
    ow_hbm,
    wg_hbm,
    wu_hbm,
    wd_hbm,
    out_ref,
    wg,
    wu,
    wd,
    keys,
    vals,
    nvals,
    qa,
    ow,
    rt,
    pk_send,
    pk_recv,
    st_send,
    st_recv,
    turned,
    att,
    part,
    part_recv,
    res_t,
    hidden,
    hid_t,
    sq,
    fac,
    frows,
    tab,
    codes,
    tok,
    pick,
    pickg,
    x,
    gu,
    r1,
    s2,
    r2,
    inner,
    ys,
    acc,
    mix,
    mix_recv,
    tsend,
    trecv,
    w_sem,
    ssem,
    rsem,
    gssem,
    grsem,
):
    reqs, ctxs, tps, block, heads, hd, exp_dev, slots, ff, share = dims
    r, c, t = lax.axis_index("req"), lax.axis_index("ctx"), lax.axis_index("tp")
    blocks = reqs * ctxs
    tokens = blocks * block
    chunk = exp_dev * slots // CHUNKS
    quarter = chunk // ctxs
    rb = min(slots, quarter)
    y, k = c // 2, c % 2
    count = [0]

    def remote(src, dst, send, recv, where):
        return pltpu.make_async_remote_copy(
            src_ref=src,
            dst_ref=dst,
            send_sem=send,
            recv_sem=recv,
            device_id={"req": r, "ctx": c, "tp": t} | where,
            device_id_type=pl.DeviceIdType.MESH,
        )

    def rcopy(src, dst, **where):
        i = count[0]
        count[0] = i + 1
        return remote(src, dst, ssem.at[i], rsem.at[i], where)

    def step(me, d, n):
        return lax.rem(me + d, n)

    cache_dev = ck_hbm.shape[0]
    rows = heads * block
    fresh = pl.ds(pl.multiple_of(c * block, block), block)
    loads = [
        pltpu.make_async_copy(src, dst, w_sem.at[i])
        for i, (src, dst) in enumerate(
            [
                (q_hbm, qa.at[:, 0:hd]),
                (ck_hbm, keys.at[0:cache_dev, 0:hd]),
                (nk_hbm.at[fresh], keys.at[cache_dev : cache_dev + block, 0:hd]),
                (cv_hbm, vals),
                (nv_hbm.at[fresh], nvals),
                (ow_hbm, ow),
                (wg_hbm, wg),
                (wu_hbm, wu),
                (wd_hbm, wd),
            ]
        )
    ]
    for load in loads[:6]:
        load.start()

    barrier = pltpu.get_barrier_semaphore()
    peers = [
        {"req": step(r, a, reqs), "ctx": step(c, b, ctxs), "tp": t}
        for a in range(reqs)
        for b in range(ctxs)
        if a or b
    ] + [{"req": r, "ctx": c, "tp": step(t, d, tps)} for d in range(1, tps)]
    swap = {"ctx": t, "tp": c}
    across = [{"req": r, "ctx": step(c, d, ctxs), "tp": c} for d in range(1, ctxs)] + [
        {"req": r, "ctx": t, "tp": step(t, d, tps)} for d in range(1, tps)
    ]

    def greet(peer):
        pl.semaphore_signal(barrier, 1, device_id=peer, device_id_type=pl.DeviceIdType.MESH)

    for peer in peers:
        greet(peer)

    @pl.when(c != t)
    def _():
        for peer in across:
            greet(peer)
        pl.semaphore_wait(barrier, len(peers) + len(across))

    @pl.when(c == t)
    def _():
        pl.semaphore_wait(barrier, len(peers))

    pending = []

    me = r * ctxs + c
    res_copy = rcopy(res_ref, res_t, **swap)

    @pl.when(c != t)
    def _():
        res_copy.start()

    @pl.when(c == t)
    def _():
        res_t[...] = res_ref[...]

    length = len_ref[r]
    scale = hd**-0.5
    lean = scale * 1.4426950408889634
    wide = keys.shape[1]
    old_at = lax.broadcasted_iota(jnp.int32, (cache_dev, wide - hd), 0)
    lane_at = lax.broadcasted_iota(jnp.int32, (cache_dev, wide - hd), 1)
    hide = jnp.logical_and(old_at >= length - c * cache_dev, lane_at == 0)
    keys[0:cache_dev, hd:wide] = jnp.where(hide, MASKED, 0.0).astype(BF16)
    qa[:, hd:wide] = jnp.ones((ctxs * rows, wide - hd), BF16)
    new_at = lax.broadcasted_iota(jnp.int32, (block, rows), 0) + c * block
    tok_at = lax.broadcasted_iota(jnp.int32, (block, rows), 1) // heads
    stat_at = lax.broadcasted_iota(jnp.int32, (8, rows), 0)
    for load in loads[:5]:
        load.wait()
    for load in loads[6:]:
        load.start()
    tile = cache_dev // 4
    pk_copies = []
    tab_copies = []
    for d in list(range(1, ctxs)) + [0]:
        b = step(c, d, ctxs)
        at = pl.ds(pl.multiple_of(b * rows, rows), rows)
        scores = [
            dot(keys[i : i + tile, :], qa[at, :], ((1,), (1,))) for i in range(0, cache_dev, tile)
        ]
        new = dot(keys[cache_dev : cache_dev + block, 0:hd], qa[at, 0:hd], ((1,), (1,)))
        scores.append(jnp.where(new_at <= tok_at + b * block, new, MASKED))
        tops = [jnp.max(s, 0, keepdims=True) for s in scores]
        top = jnp.maximum(functools.reduce(jnp.maximum, tops), -1e28)
        total, sums = None, None
        for i, s in enumerate(scores):
            w = jnp.exp2((s - top) * lean)
            v = vals[i * tile : (i + 1) * tile, :] if i * tile < cache_dev else nvals[...]
            part_total = jnp.sum(w, 0, keepdims=True)
            part_sums = dot(v, w.astype(BF16), ((0,), (0,)))
            total = part_total if total is None else total + part_total
            sums = part_sums if sums is None else sums + part_sums
        pk_send[d] = sums.astype(BF16)
        st_send[d] = jnp.where(
            stat_at == 0, top * scale, jnp.where(stat_at == 1, total, 0.0)
        )
        if d:
            for src, dst in ((pk_send, pk_recv), (st_send, st_recv)):
                copy = rcopy(src.at[d], dst.at[d], ctx=b)
                copy.start()
                pk_copies.append(copy)
        if d == 1:
            n_exp = reqs * exp_dev
            ids = jnp.concatenate([ids_ref[...]] * (128 // block), 1)
            gws = jnp.concatenate([gw_ref[...]] * (128 // block), 1)
            half = lax.broadcasted_iota(jnp.int32, ids.shape, 1) // block
            ids = jnp.where(half == lax.rem(me, 128 // block), ids, -1)
            exp_at = lax.broadcasted_iota(jnp.int32, (n_exp, 128), 0)
            hit = jnp.zeros((n_exp, 128), F32)
            gates = jnp.zeros((n_exp, 128), F32)
            for route in range(TOP):
                same = ids[route : route + 1, :] == exp_at
                hit = hit + jnp.where(same, 1.0, 0.0)
                gates = gates + jnp.where(same, gws[route : route + 1, :], 0.0)
            one_at = lax.broadcasted_iota(jnp.int32, (128, 128), 0)
            two_at = lax.broadcasted_iota(jnp.int32, (128, 128), 1)
            upto = jnp.where(one_at <= two_at, 1.0, 0.0).astype(BF16)
            rank = dot(hit.astype(BF16), upto, ((1,), (0,)))
            code = jnp.where(hit > 0.0, rank + (me * CAP).astype(F32), 0.0)
            for a in range(reqs):
                rt[a, 0:exp_dev, :] = code[a * exp_dev : (a + 1) * exp_dev]
                rt[a, exp_dev : 2 * exp_dev, :] = gates[a * exp_dev : (a + 1) * exp_dev]
            for a in range(reqs):
                for b2 in range(ctxs):
                    if a or b2:
                        to = step(r, a, reqs)
                        copy = rcopy(rt.at[to], tab.at[me], req=to, ctx=step(c, b2, ctxs))
                        copy.start()
                        tab_copies.append(copy)
            tab[me] = rt[r]
    for copy in pk_copies:
        copy.wait_recv()
    pending += pk_copies
    packs = [pk_send[0]] + [pk_recv[d] for d in range(1, ctxs)]
    stats = [st_send[0]] + [st_recv[d] for d in range(1, ctxs)]
    tops = [st[0:1, :] for st in stats]
    top = functools.reduce(jnp.maximum, tops)
    total = jnp.zeros((1, rows), F32)
    sums = jnp.zeros((hd, rows), F32)
    for p, st, own in zip(packs, stats, tops):
        factor = jnp.exp(own - top)
        total = total + factor * st[1:2, :]
        sums = sums + factor * p.astype(F32)
    turned[...] = jnp.transpose(sums / total)
    for h in range(heads):
        att[c, :, h * hd : (h + 1) * hd] = turned[pl.ds(h, block, stride=heads), :].astype(BF16)
    att_copies = []
    for d in range(1, ctxs):
        copy = rcopy(att.at[c], att.at[c], ctx=step(c, d, ctxs))
        copy.start()
        att_copies.append(copy)
    for copy in tab_copies:
        copy.wait_recv()
    pending += tab_copies
    for p in range(blocks // 2):
        codes[:, p * 128 : (p + 1) * 128] = tab[2 * p] + tab[2 * p + 1]
    slot_at = lax.broadcasted_iota(jnp.int32, (rb, tokens), 0).astype(F32)

    def make_pick(i, carry):
        row = i * rb
        e = row // slots
        at = pl.ds(pl.multiple_of(row, rb), rb)
        code = codes[pl.ds(e, 1), :] - (row - e * slots + 1).astype(F32)
        mine = slot_at == code
        pick[at, :] = jnp.where(mine, 1.0, 0.0).astype(BF16)
        pickg[at, :] = jnp.where(mine, codes[pl.ds(exp_dev + e, 1), :], 0.0).astype(BF16)
        return carry

    lax.fori_loop(0, exp_dev * slots // rb, make_pick, 0)
    loads[5].wait()
    for copy in att_copies:
        copy.wait_recv()
    pending += att_copies
    width = heads * hd
    full = dot(att[...].reshape(ctxs * block, width), ow[...], ((1,), (0,)))
    part[...] = full.reshape(tps, block, share).astype(BF16)
    part_copies = []
    for d in range(1, tps):
        to = step(t, d, tps)
        copy = rcopy(part.at[to], part_recv.at[d], tp=to)
        copy.start()
        part_copies.append(copy)
    hid = part[t].astype(F32)

    @pl.when(c != t)
    def _():
        res_copy.wait_recv()

    hid = hid + res_t[...].astype(F32)
    for d in range(1, tps):
        part_copies[d - 1].wait_recv()
        hid = hid + part_recv[d].astype(F32)
    pending += part_copies
    hidden[...] = hid
    lanes = share // 128
    mine = r * tps + t
    for q in range(lanes):
        sl = slice(q * 128, (q + 1) * 128)
        tok[mine, :, sl] = (hid[:, sl] * gain_ref[pl.ds(c * lanes + q, 1), :]).astype(BF16)
    tok_copies = []
    for d in range(1, tps):
        copy = rcopy(tok.at[mine], tok.at[mine], tp=step(t, d, tps))
        copy.start()
        tok_copies.append(copy)
    far_copies = []
    for a in range(1, reqs):
        copy = rcopy(tok.at[mine], tok.at[mine], req=step(r, a, reqs))
        copy.start()
        far_copies.append(copy)
    squares = jnp.broadcast_to(jnp.sum(hid * hid, 1, keepdims=True), (block, 128))
    squares = jnp.concatenate([squares] * (128 // block), 0)
    sq[0] = jnp.transpose(squares)[0:8]
    sq_copies = []
    for d in range(1, ctxs):
        copy = rcopy(sq.at[0], sq.at[d], ctx=step(c, d, ctxs))
        copy.start()
        sq_copies.append(copy)
    for copy in sq_copies:
        copy.wait_recv()
    pending += sq_copies
    squares = sq[0]
    for d in range(1, ctxs):
        squares = squares + sq[d]
    fac[mine] = lax.rsqrt(squares / (share * ctxs) + 1e-6)
    fac_copies = []
    for d in range(1, tps):
        copy = rcopy(fac.at[mine], fac.at[mine], tp=step(t, d, tps))
        copy.start()
        fac_copies.append(copy)
    fac_far = []
    for a in range(1, reqs):
        copy = rcopy(fac.at[mine], fac.at[mine], req=step(r, a, reqs))
        copy.start()
        fac_far.append(copy)
    for d in range(1, tps):
        tok_copies[d - 1].wait_recv()
        at = r * tps + step(t, tps - d, tps)
        for a in range(1, reqs):
            copy = rcopy(tok.at[at], tok.at[at], req=step(r, a, reqs))
            copy.start()
            far_copies.append(copy)
    hid_copy = rcopy(hidden, hid_t, **swap)

    @pl.when(c != t)
    def _():
        hid_copy.start()

    @pl.when(c == t)
    def _():
        hid_t[...] = hidden[...]

    for d in range(1, tps):
        fac_copies[d - 1].wait_recv()
        at = r * tps + step(t, tps - d, tps)
        for a in range(1, reqs):
            copy = rcopy(fac.at[at], fac.at[at], req=step(r, a, reqs))
            copy.start()
            fac_far.append(copy)
    for load in loads[6:8]:
        load.wait()
    for copy in far_copies:
        copy.wait_recv()
    pending += tok_copies + far_copies + fac_copies

    n_sub = chunk // rb
    n_q = quarter // rb
    first, second, third, fourth = [], [], [], []

    def up_stage(j):
        base = j * chunk
        x[...] = dot(
            pick[base : base + chunk, :], tok[...].reshape(tokens, share), ((1,), (0,))
        ).astype(BF16)

        def one(i, carry):
            e = (base + i * rb) // slots
            at = pl.ds(pl.multiple_of((i % n_q) * rb, rb), rb)
            xs = x[pl.ds(pl.multiple_of(i * rb, rb), rb), :]
            q = i // n_q
            gu[0, j, q // 2, q % 2, at, :] = dot(xs, wg[e], ((1,), (1,))).astype(BF16)
            gu[1, j, q // 2, q % 2, at, :] = dot(xs, wu[e], ((1,), (1,))).astype(BF16)
            return carry

        lax.fori_loop(0, n_sub, one, 0, unroll=min(4, n_sub))
        copy = rcopy(gu.at[:, j, :, 1 - k], r1.at[:, j], ctx=y * 2 + 1 - k)
        copy.start()
        first.append(copy)

    def pair_stage(j):
        first[j].wait_recv()
        s2[:, j] = (
            gu[:, j, 1 - y, k].astype(F32) + r1[:, j, 1 - y].astype(F32)
        ).astype(BF16)
        copy = rcopy(s2.at[:, j], r2.at[:, j], ctx=(1 - y) * 2 + k)
        copy.start()
        second.append(copy)

    def factor_rows():
        low_lane = lax.broadcasted_iota(jnp.int32, (8, 128), 1) < block
        row_at = lax.broadcasted_iota(jnp.int32, (8, 128), 0)
        for p in range(blocks // 2):
            f = jnp.where(low_lane, fac[2 * p], fac[2 * p + 1])
            hi = f.astype(BF16).astype(F32)
            mid = (f - hi).astype(BF16).astype(F32)
            low = f - hi - mid
            f = jnp.where(row_at == 0, hi, jnp.where(row_at == 1, mid, low))
            frows[:, p * 128 : (p + 1) * 128] = jnp.where(row_at < 3, f, 0.0)

    def act_stage(j):
        second[j].wait_recv()
        both = gu[:, j, y, k].astype(F32) + r1[:, j, y].astype(F32) + r2[:, j].astype(F32)
        mine = pick[pl.ds(pl.multiple_of(j * chunk + c * quarter, quarter), quarter), :]
        row = jnp.sum(dot(mine, frows[...].astype(BF16), ((1,), (1,))), 1, keepdims=True)
        g = both[0] * row
        inner[j, y, k] = (g * jax.nn.sigmoid(g) * (both[1] * row)).astype(BF16)
        copy = rcopy(inner.at[j, y, k], inner.at[j, y, k], ctx=(1 - y) * 2 + k)
        copy.start()
        third.append(copy)

    def share_stage(j):
        third[j].wait_recv()
        copy = rcopy(inner.at[j, :, k], inner.at[j, :, k], ctx=y * 2 + 1 - k)
        copy.start()
        fourth.append(copy)

    def down_stage(j, at_col, cols):
        base = j * chunk
        sl = slice(at_col, at_col + cols)

        def one(i, carry):
            e = (base + i * rb) // slots
            q = i // n_q
            at = pl.ds(pl.multiple_of((i % n_q) * rb, rb), rb)
            rows_at = pl.multiple_of(i * rb, rb)
            down = dot(inner[j, q // 2, q % 2, at, :], wd[e, :, sl], ((1,), (0,)))
            ys[pl.ds(rows_at, rb), sl] = down.astype(BF16)
            return carry

        lax.fori_loop(0, n_sub, one, 0, unroll=min(4, n_sub))
        term = dot(pickg[base : base + chunk, :], ys[:, sl], ((0,), (0,)))
        if j == 0:
            acc[:, sl] = term
        else:
            acc[:, sl] += term

    up_stage(0)
    up_stage(1)
    pair_stage(0)
    up_stage(2)
    for copy in fac_far:
        copy.wait_recv()
    pending.extend(fac_far)
    factor_rows()
    act_stage(0)
    pair_stage(1)
    up_stage(3)
    loads[8].wait()
    share_stage(0)
    act_stage(1)
    pair_stage(2)
    fourth[0].wait_recv()
    down_stage(0, 0, share)
    share_stage(1)
    act_stage(2)
    pair_stage(3)
    fourth[1].wait_recv()
    down_stage(1, 0, share)
    share_stage(2)
    act_stage(3)
    fourth[2].wait_recv()
    down_stage(2, 0, share)
    share_stage(3)
    fourth[3].wait_recv()
    pending += first + second + third + fourth

    per = tps * block
    cols = share // PIECES
    mix_copies = []
    for piece in range(PIECES):
        sl = slice(piece * cols, (piece + 1) * cols)
        down_stage(CHUNKS - 1, piece * cols, cols)
        for a in range(1, reqs):
            to = step(r, a, reqs)
            at = pl.ds(pl.multiple_of(to * per, per), per)
            mix[piece, a] = acc[at, sl].astype(BF16)
            copy = rcopy(mix.at[piece, a], mix_recv.at[piece, a], req=to)
            copy.start()
            mix_copies.append(copy)
    pending += mix_copies
    for piece in range(PIECES):
        sl = slice(piece * cols, (piece + 1) * cols)
        mixed = acc[pl.ds(pl.multiple_of(r * per, per), per), sl]
        for a in range(1, reqs):
            mix_copies[piece * (reqs - 1) + a - 1].wait_recv()
            mixed = mixed + mix_recv[piece, a].astype(F32)
        tsend[piece] = mixed.reshape(tps, block, cols).astype(BF16)
        for d in range(1, ctxs):
            to = step(c, d, ctxs)
            copy = remote(
                tsend.at[piece, to],
                trecv.at[piece, t],
                gssem.at[piece, d],
                grsem.at[piece, t],
                {"ctx": to, "tp": c},
            )
            copy.start()
            pending.append(copy)

        @pl.when(c != t)
        def _():
            remote(
                tsend.at[piece, c],
                trecv.at[piece, t],
                gssem.at[piece, 0],
                grsem.at[piece, t],
                {"tp": c},
            ).start()

        @pl.when(c == t)
        def _():
            trecv[piece, t] = tsend[piece, c]

    @pl.when(c != t)
    def _():
        hid_copy.wait_recv()

    for piece in range(PIECES):
        sl = slice(piece * cols, (piece + 1) * cols)

        def arrival(d):
            at = step(t, d, tps)
            return remote(
                tsend.at[piece, 0],
                trecv.at[piece, at],
                gssem.at[piece, 0],
                grsem.at[piece, at],
                {"ctx": step(c, 1, ctxs)},
            )

        @pl.when(c != t)
        def _():
            arrival(0).wait_recv()

        total = hid_t[:, sl] + trecv[piece, t].astype(F32)
        for d in range(1, tps):
            arrival(d).wait_recv()
            total = total + trecv[piece, step(t, d, tps)].astype(F32)
        out_ref[:, sl] = total.astype(BF16)

    @pl.when(c != t)
    def _():
        res_copy.wait_send()
        hid_copy.wait_send()
        for piece in range(PIECES):
            remote(
                tsend.at[piece, c],
                trecv.at[piece, t],
                gssem.at[piece, 0],
                grsem.at[piece, t],
                {"tp": c},
            ).wait_send()

    for copy in pending:
        copy.wait_send()


def fused_body(
    queries,
    new_keys,
    new_values,
    cache_keys,
    cache_values,
    cache_lengths,
    residual,
    out_weight,
    norm_gain,
    expert_ids,
    gate_weights,
    w_gate,
    w_up,
    w_down,
):
    reqs, ctxs, tps = (lax.axis_size(a) for a in ("req", "ctx", "tp"))
    tok_dev, heads, hd = queries.shape
    block, share = residual.shape
    exp_dev, _, ff = w_gate.shape
    cache_dev = cache_keys.shape[1]
    blocks = reqs * ctxs
    slots = blocks * CAP
    tokens = blocks * block
    chunk = exp_dev * slots // CHUNKS
    quarter = chunk // ctxs
    rows = heads * block
    per, cols = tps * block, share // PIECES
    dims = (reqs, ctxs, tps, block, heads, hd, exp_dev, slots, ff, share)
    n_rem = (
        (blocks - 1)
        + 2
        + 3 * (ctxs - 1)
        + (tps - 1)
        + (ctxs - 1)
        + 2 * (tps - 1)
        + 2 * tps * (reqs - 1)
        + 4 * CHUNKS
        + PIECES * (reqs - 1)
    )
    vmem = pl.BlockSpec(memory_space=pltpu.VMEM)
    anywhere = pl.BlockSpec(memory_space=pl.ANY)
    scratch = [
        ((exp_dev, ff, share), BF16),
        ((exp_dev, ff, share), BF16),
        ((exp_dev, ff, share), BF16),
        ((cache_dev + block, hd + 128), BF16),
        ((cache_dev, hd), BF16),
        ((block, hd), BF16),
        ((ctxs * rows, hd + 128), BF16),
        ((heads * hd, share), BF16),
        ((reqs, 2 * exp_dev, 128), F32),
        ((ctxs, hd, rows), BF16),
        ((ctxs, hd, rows), BF16),
        ((ctxs, 8, rows), F32),
        ((ctxs, 8, rows), F32),
        ((rows, hd), F32),
        ((ctxs, block, heads * hd), BF16),
        ((tps, block, share), BF16),
        ((tps, block, share), BF16),
        ((block, share), BF16),
        ((block, share), F32),
        ((block, share), F32),
        ((ctxs, 8, 128), F32),
        ((reqs * tps, 8, 128), F32),
        ((8, tokens), F32),
        ((blocks, 2 * exp_dev, 128), F32),
        ((2 * exp_dev, tokens), F32),
        ((reqs * tps, block, share), BF16),
        ((exp_dev * slots, tokens), BF16),
        ((exp_dev * slots, tokens), BF16),
        ((chunk, share), BF16),
        ((2, CHUNKS, 2, 2, quarter, ff), BF16),
        ((2, CHUNKS, 2, quarter, ff), BF16),
        ((2, CHUNKS, quarter, ff), BF16),
        ((2, CHUNKS, quarter, ff), BF16),
        ((CHUNKS, 2, 2, quarter, ff), BF16),
        ((chunk, share), BF16),
        ((tokens, share), F32),
        ((PIECES, reqs, per, cols), BF16),
        ((PIECES, reqs, per, cols), BF16),
        ((PIECES, tps, block, cols), BF16),
        ((PIECES, tps, block, cols), BF16),
    ]
    return pl.pallas_call(
        functools.partial(layer_kernel, dims),
        out_shape=jax.ShapeDtypeStruct((block, share), BF16),
        in_specs=[pl.BlockSpec(memory_space=pltpu.SMEM)] + [vmem] * 4 + [anywhere] * 9,
        out_specs=vmem,
        scratch_shapes=[pltpu.VMEM(*s) for s in scratch]
        + [
            pltpu.SemaphoreType.DMA((9,)),
            pltpu.SemaphoreType.DMA((n_rem,)),
            pltpu.SemaphoreType.DMA((n_rem,)),
            pltpu.SemaphoreType.DMA((PIECES, ctxs)),
            pltpu.SemaphoreType.DMA((PIECES, tps)),
        ],
        compiler_params=pltpu.CompilerParams(
            collective_id=0, has_side_effects=True, vmem_limit_bytes=63 * 1024 * 1024
        ),
    )(
        cache_lengths,
        expert_ids.T,
        gate_weights.T,
        norm_gain.reshape(-1, 128),
        residual,
        queries.reshape(tok_dev * heads, hd),
        cache_keys[0, :, 0, :],
        cache_values[0, :, 0, :],
        new_keys[:, 0, :],
        new_values[:, 0, :],
        out_weight,
        jnp.swapaxes(w_gate, 1, 2),
        jnp.swapaxes(w_up, 1, 2),
        w_down,
    )


def attention_part(queries, new_keys, new_values, cache_keys, cache_values, length):
    ctx_pos, ctx_count = lax.axis_index("ctx"), lax.axis_size("ctx")
    tok_dev, heads, hd = queries.shape
    cache_dev = cache_keys.shape[1]
    block = tok_dev // ctx_count
    rows = heads * block
    q = queries.reshape(ctx_count, block, heads, hd).transpose(0, 2, 1, 3)
    q = q.reshape(ctx_count * rows, hd)
    keys = jnp.concatenate([cache_keys[0, :, 0, :], new_keys[:, 0, :]], 0)
    values = jnp.concatenate([cache_values[0, :, 0, :], new_values[:, 0, :]], 0)
    scores = jnp.dot(keys, q.T, preferred_element_type=jnp.float32) * (hd**-0.5)
    key_at = jnp.arange(cache_dev + tok_dev, dtype=jnp.int32)[:, None]
    row_at = jnp.arange(ctx_count * rows, dtype=jnp.int32)[None, :]
    token = (row_at // rows) * block + row_at % block
    valid = jnp.where(
        key_at < cache_dev,
        ctx_pos * cache_dev + key_at < length,
        jnp.logical_and(ctx_pos == ctx_count - 1, key_at - cache_dev <= token),
    )
    scores = jnp.where(valid, scores, MASKED)
    top = jnp.max(scores, 0, keepdims=True)
    weights = jnp.where(valid, jnp.exp(scores - top), 0.0)
    total = jnp.sum(weights, 0, keepdims=True)
    sums = lax.dot_general(
        values,
        weights.astype(jnp.bfloat16),
        (((0,), (0,)), ((), ())),
        preferred_element_type=jnp.float32,
    )
    pack = jnp.concatenate([sums, top, total, jnp.zeros((6, ctx_count * rows), jnp.float32)], 0)
    return pack.reshape(hd + 8, ctx_count, rows).transpose(1, 0, 2)


def merge(packs, hd, heads):
    top = jnp.max(packs[:, hd : hd + 1], 0)
    factor = jnp.exp(packs[:, hd : hd + 1] - top)
    total = jnp.sum(factor * packs[:, hd + 1 : hd + 2], 0)
    out = (jnp.sum(factor * packs[:, :hd], 0) / total).astype(jnp.bfloat16)
    block = out.shape[1] // heads
    return out.reshape(hd, heads, block).transpose(2, 1, 0).reshape(block, heads * hd)


def route_tables(expert_ids, gate_weights, exp_dev):
    block = expert_ids.shape[0]
    both = jnp.concatenate([expert_ids.astype(jnp.float32), gate_weights], 1)
    both = lax.all_gather(both, ("req", "ctx"))
    blocks = both.shape[0]
    ids = both[:, :, :TOP].astype(jnp.int32)
    gates = both[:, :, TOP:]
    first = lax.axis_index("req") * exp_dev
    experts = first + jnp.arange(exp_dev, dtype=jnp.int32)
    hits = ids[:, :, :, None] == experts
    gate_at = jnp.sum(jnp.where(hits, gates[..., None], 0.0), 2)
    hit = jnp.any(hits, 2)
    earlier = jnp.tril(jnp.ones((block, block), jnp.bfloat16), -1)
    rank = jnp.einsum(
        "ij,bje->bie", earlier, hit.astype(jnp.bfloat16), preferred_element_type=jnp.float32
    )
    code = jnp.arange(blocks, dtype=jnp.int32)[:, None, None] * CAP + rank.astype(jnp.int32)
    code = jnp.where(hit, code, -1)
    flat = (blocks * block, exp_dev)
    return code.reshape(flat).T, gate_at.reshape(flat).T


def spread_body(
    queries,
    new_keys,
    new_values,
    cache_keys,
    cache_values,
    cache_lengths,
    residual,
    out_weight,
    norm_gain,
    expert_ids,
    gate_weights,
    w_gate,
    w_up,
    w_down,
):
    ctx_pos, tp_pos, req_pos = (lax.axis_index(a) for a in ("ctx", "tp", "req"))
    ctx_count, req_count = lax.axis_size("ctx"), lax.axis_size("req")
    tok_dev, heads, hd = queries.shape
    block, share = residual.shape
    exp_dev = w_gate.shape[0]
    slots = req_count * ctx_count * CAP
    length = lax.dynamic_index_in_dim(cache_lengths, req_pos, 0, keepdims=False)
    code, gate_at = route_tables(expert_ids, gate_weights, exp_dev)
    swap = [(a * ctx_count + b, b * ctx_count + a) for a in range(ctx_count) for b in range(ctx_count)]
    residual_t = lax.ppermute(residual, ("ctx", "tp"), swap)
    packs = attention_part(queries, new_keys, new_values, cache_keys, cache_values, length)
    packs = lax.all_to_all(packs, "ctx", 0, 0, tiled=True)
    attended = merge(packs, hd, heads)
    attended = lax.all_gather(attended, "ctx", tiled=True)
    part = jnp.dot(attended, out_weight, preferred_element_type=jnp.float32)
    part = part.reshape(-1, block, share)
    part = lax.all_to_all(part, "tp", 0, 0, tiled=True)
    hidden = jnp.sum(part, 0) + residual_t.astype(jnp.float32)
    squares = jnp.sum(hidden * hidden, 1)
    gain = lax.dynamic_slice_in_dim(norm_gain, ctx_pos * share, share, 0)
    scaled = (hidden * gain).astype(jnp.bfloat16)
    squares = lax.psum(squares, "ctx")
    factor = lax.rsqrt(squares / norm_gain.shape[0] + 1e-6)
    factor = lax.all_gather(factor, ("req", "tp"), tiled=True)
    scaled = lax.all_gather(scaled, ("req", "tp"), tiled=True)
    pick = code[:, None, :] == jnp.arange(slots, dtype=jnp.int32)[None, :, None]
    row_factor = jnp.sum(jnp.where(pick, factor, 0.0), -1, keepdims=True)
    row_gate = jnp.sum(jnp.where(pick, gate_at[:, None, :], 0.0), -1, keepdims=True)
    pick = pick.astype(jnp.bfloat16)
    rows = jnp.einsum("est,td->esd", pick, scaled, preferred_element_type=jnp.bfloat16)
    gate = jnp.einsum("esd,edf->esf", rows, w_gate, preferred_element_type=jnp.float32)
    up = jnp.einsum("esd,edf->esf", rows, w_up, preferred_element_type=jnp.float32)
    both = jnp.stack([gate, up], 2).astype(jnp.bfloat16)
    both = both.reshape(ctx_count, exp_dev * slots // ctx_count, 2, -1)
    both = lax.all_to_all(both, "ctx", 0, 0, tiled=True)
    both = both.astype(jnp.float32).sum(0)
    per = exp_dev * slots // ctx_count
    mine = lax.dynamic_slice_in_dim(row_factor.reshape(-1, 1), ctx_pos * per, per, 0)
    inner = (jax.nn.silu(both[:, 0] * mine) * (both[:, 1] * mine)).astype(jnp.bfloat16)
    inner = lax.all_gather(inner, "ctx", tiled=True).reshape(exp_dev, slots, -1)
    down = jnp.einsum("esf,efd->esd", inner, w_down, preferred_element_type=jnp.float32)
    down = (down * row_gate).astype(jnp.bfloat16)
    mixed = jnp.einsum("est,esd->td", pick, down, preferred_element_type=jnp.float32)
    mixed = mixed.astype(jnp.bfloat16).reshape(-1, block, share)
    mixed = lax.all_to_all(mixed, ("req", "tp"), 0, 0, tiled=True)
    out = hidden + jnp.sum(mixed.astype(jnp.float32), 0)
    return lax.ppermute(out.astype(jnp.bfloat16), ("ctx", "tp"), swap)


def body(*args):
    tokens = args[0].shape[0] * lax.axis_size("req")
    slots = args[11].shape[0] * lax.axis_size("req") * lax.axis_size("ctx") * CAP
    if tokens * slots * 2 <= FUSED_BYTES:
        return fused_body(*args)
    return spread_body(*args)


def solution(mesh):
    in_specs = (
        P("req", "tp", None),
        P("req", "tp", None),
        P("req", "tp", None),
        P("req", "ctx", "tp", None),
        P("req", "ctx", "tp", None),
        P(),
        P(("req", "ctx"), "tp"),
        P("tp", "ctx"),
        P(),
        P(("req", "ctx"), None),
        P(("req", "ctx"), None),
        P("req", "ctx", "tp"),
        P("req", "ctx", "tp"),
        P("req", "tp", "ctx"),
    )
    out_specs = P(("req", "ctx"), "tp")
    return jax.shard_map(body, mesh=mesh, in_specs=in_specs, out_specs=out_specs, check_vma=False)
```

```python
import functools
import jax
import jax.numpy as jnp
from jax import lax
from jax.experimental import pallas as pl
from jax.experimental.pallas import tpu as pltpu
from jax.sharding import PartitionSpec as P

TOP = 6
CAP = 8
MASKED = -1e30
F32 = jnp.float32
BF16 = jnp.bfloat16
GROUPS = 4
PIECES = 2
HALVES = 2
ORDER = (
    "U0 P0 U1 U2",
    "P1 A0 U3 P2",
    "U4 P3 A1 U5",
    "P4 U6 A2 U7",
    "A3 S0 S1 D0",
    "A4 P5 P6 P7",
    "S2 D1 S3 D2",
    "D3 S4 D4",
    "A5 A6 A7",
    "S5 D5 S6 S7",
    "D6 D7",
)
FUSED_BYTES = 4 * 1024 * 1024


def dot(a, b, contract, kind=F32):
    return lax.dot_general(a, b, (contract, ((), ())), preferred_element_type=kind)


def layer_kernel(
    dims,
    len_ref,
    ids_ref,
    gw_ref,
    gain_ref,
    res_ref,
    q_hbm,
    ck_hbm,
    cv_hbm,
    nk_hbm,
    nv_hbm,
    ow_hbm,
    wg_hbm,
    wu_hbm,
    wd_hbm,
    out_ref,
    wg,
    wu,
    wd,
    keys,
    vals,
    nvals,
    qa,
    ow,
    rt,
    pk_send,
    pk_recv,
    st_send,
    st_recv,
    turned,
    att,
    part,
    part_recv,
    res_t,
    hidden,
    sq,
    fac,
    frows,
    tab,
    codes,
    tok,
    pick,
    pickg,
    x,
    gu,
    r1,
    s2,
    r2,
    inner,
    ys,
    acc,
    mix,
    mix_recv,
    tsend,
    trecv,
    w_sem,
    ssem,
    rsem,
    gssem,
    grsem,
    tssem,
    trsem,
    fssem,
    frsem,
):
    reqs, ctxs, tps, block, heads, hd, exp_dev, slots, ff, share = dims
    r, c, t = lax.axis_index("req"), lax.axis_index("ctx"), lax.axis_index("tp")
    blocks = reqs * ctxs
    own_toks = ctxs * block
    rb = ctxs * CAP
    members = exp_dev // GROUPS
    chunk = members * rb
    quarter = chunk // ctxs
    plan = (
        [(0, 0)]
        + [(g, a) for a in range(1, reqs) for g in range(GROUPS)]
        + [(g, 0) for g in range(1, GROUPS)]
    )
    y, k = c // 2, c % 2
    count = [0]

    def remote(src, dst, send, recv, where):
        return pltpu.make_async_remote_copy(
            src_ref=src,
            dst_ref=dst,
            send_sem=send,
            recv_sem=recv,
            device_id={"req": r, "ctx": c, "tp": t} | where,
            device_id_type=pl.DeviceIdType.MESH,
        )

    def rcopy(src, dst, **where):
        i = count[0]
        count[0] = i + 1
        return remote(src, dst, ssem.at[i], rsem.at[i], where)

    def step(me, d, n):
        return lax.rem(me + d, n)

    cache_dev = ck_hbm.shape[0]
    rows = heads * block
    fresh = pl.ds(pl.multiple_of(c * block, block), block)
    loads = [
        pltpu.make_async_copy(src, dst, w_sem.at[i])
        for i, (src, dst) in enumerate(
            [
                (q_hbm, qa.at[:, 0:hd]),
                (ck_hbm, keys.at[0:cache_dev, 0:hd]),
                (nk_hbm.at[fresh], keys.at[cache_dev : cache_dev + block, 0:hd]),
                (cv_hbm, vals),
                (nv_hbm.at[fresh], nvals),
                (ow_hbm, ow),
                (wg_hbm, wg),
                (wu_hbm, wu),
                (wd_hbm, wd),
            ]
        )
    ]
    for load in loads[:6]:
        load.start()

    barrier = pltpu.get_barrier_semaphore()
    peers = [
        {"req": step(r, a, reqs), "ctx": step(c, b, ctxs), "tp": t}
        for a in range(reqs)
        for b in range(ctxs)
        if a or b
    ] + [
        {"req": step(r, a, reqs), "ctx": c, "tp": step(t, d, tps)}
        for a in range(reqs)
        for d in range(1, tps)
    ]
    swap = {"ctx": t, "tp": c}
    across = [{"req": r, "ctx": step(c, d, ctxs), "tp": c} for d in range(1, ctxs)] + [
        {"req": r, "ctx": t, "tp": step(t, d, tps)} for d in range(1, tps)
    ]

    def greet(peer):
        pl.semaphore_signal(barrier, 1, device_id=peer, device_id_type=pl.DeviceIdType.MESH)

    for peer in peers:
        greet(peer)

    @pl.when(c != t)
    def _():
        for peer in across:
            greet(peer)
        pl.semaphore_wait(barrier, len(peers) + len(across))

    @pl.when(c == t)
    def _():
        pl.semaphore_wait(barrier, len(peers))

    pending = []

    me = r * ctxs + c
    res_copy = rcopy(res_ref, res_t, **swap)

    @pl.when(c != t)
    def _():
        res_copy.start()

    @pl.when(c == t)
    def _():
        res_t[...] = res_ref[...]

    length = len_ref[r]
    scale = hd**-0.5
    lean = scale * 1.4426950408889634
    wide = keys.shape[1]
    old_at = lax.broadcasted_iota(jnp.int32, (cache_dev, wide - hd), 0)
    lane_at = lax.broadcasted_iota(jnp.int32, (cache_dev, wide - hd), 1)
    hide = jnp.logical_and(old_at >= length - c * cache_dev, lane_at == 0)
    keys[0:cache_dev, hd:wide] = jnp.where(hide, MASKED, 0.0).astype(BF16)
    qa[:, hd:wide] = jnp.ones((ctxs * rows, wide - hd), BF16)
    new_at = lax.broadcasted_iota(jnp.int32, (block, rows), 0) + c * block
    tok_at = lax.broadcasted_iota(jnp.int32, (block, rows), 1) // heads
    stat_at = lax.broadcasted_iota(jnp.int32, (8, rows), 0)
    for load in loads[:5]:
        load.wait()
    for load in loads[6:]:
        load.start()
    tile = cache_dev // 4
    pk_copies = []
    tab_copies = []
    for d in list(range(1, ctxs)) + [0]:
        b = step(c, d, ctxs)
        at = pl.ds(pl.multiple_of(b * rows, rows), rows)
        scores = [
            dot(keys[i : i + tile, :], qa[at, :], ((1,), (1,))) for i in range(0, cache_dev, tile)
        ]
        new = dot(keys[cache_dev : cache_dev + block, 0:hd], qa[at, 0:hd], ((1,), (1,)))
        scores.append(jnp.where(new_at <= tok_at + b * block, new, MASKED))
        tops = [jnp.max(s, 0, keepdims=True) for s in scores]
        top = jnp.maximum(functools.reduce(jnp.maximum, tops), -1e28)
        total, sums = None, None
        for i, s in enumerate(scores):
            w = jnp.exp2((s - top) * lean)
            v = vals[i * tile : (i + 1) * tile, :] if i * tile < cache_dev else nvals[...]
            part_total = jnp.sum(w, 0, keepdims=True)
            part_sums = dot(v, w.astype(BF16), ((0,), (0,)))
            total = part_total if total is None else total + part_total
            sums = part_sums if sums is None else sums + part_sums
        pk_send[d] = sums.astype(BF16)
        st_send[d] = jnp.where(
            stat_at == 0, top * scale, jnp.where(stat_at == 1, total, 0.0)
        )
        if d:
            for src, dst in ((pk_send, pk_recv), (st_send, st_recv)):
                copy = rcopy(src.at[d], dst.at[d], ctx=b)
                copy.start()
                pk_copies.append(copy)
        if d == 1:
            n_exp = reqs * exp_dev
            ids = jnp.concatenate([ids_ref[...]] * (128 // block), 1)
            gws = jnp.concatenate([gw_ref[...]] * (128 // block), 1)
            half = lax.broadcasted_iota(jnp.int32, ids.shape, 1) // block
            ids = jnp.where(half == lax.rem(me, 128 // block), ids, -1)
            exp_at = lax.broadcasted_iota(jnp.int32, (n_exp, 128), 0)
            hit = jnp.zeros((n_exp, 128), F32)
            gates = jnp.zeros((n_exp, 128), F32)
            for route in range(TOP):
                same = ids[route : route + 1, :] == exp_at
                hit = hit + jnp.where(same, 1.0, 0.0)
                gates = gates + jnp.where(same, gws[route : route + 1, :], 0.0)
            one_at = lax.broadcasted_iota(jnp.int32, (128, 128), 0)
            two_at = lax.broadcasted_iota(jnp.int32, (128, 128), 1)
            upto = jnp.where(one_at <= two_at, 1.0, 0.0).astype(BF16)
            rank = dot(hit.astype(BF16), upto, ((1,), (0,)))
            code = jnp.where(hit > 0.0, rank + (c * CAP).astype(F32), 0.0)
            for a in range(reqs):
                rt[a, 0:exp_dev, :] = code[a * exp_dev : (a + 1) * exp_dev]
                rt[a, exp_dev : 2 * exp_dev, :] = gates[a * exp_dev : (a + 1) * exp_dev]
            for a in range(reqs):
                for b2 in range(ctxs):
                    if a or b2:
                        to = step(r, a, reqs)
                        copy = rcopy(rt.at[to], tab.at[me], req=to, ctx=step(c, b2, ctxs))
                        copy.start()
                        tab_copies.append(copy)
            tab[me] = rt[r]
    for copy in pk_copies:
        copy.wait_recv()
    pending += pk_copies
    packs = [pk_send[0]] + [pk_recv[d] for d in range(1, ctxs)]
    stats = [st_send[0]] + [st_recv[d] for d in range(1, ctxs)]
    tops = [st[0:1, :] for st in stats]
    top = functools.reduce(jnp.maximum, tops)
    total = jnp.zeros((1, rows), F32)
    sums = jnp.zeros((hd, rows), F32)
    for p, st, own in zip(packs, stats, tops):
        factor = jnp.exp(own - top)
        total = total + factor * st[1:2, :]
        sums = sums + factor * p.astype(F32)
    turned[...] = jnp.transpose(sums / total)
    for h in range(heads):
        att[c, :, h * hd : (h + 1) * hd] = turned[pl.ds(h, block, stride=heads), :].astype(BF16)
    att_copies = []
    for d in range(1, ctxs):
        copy = rcopy(att.at[c], att.at[c], ctx=step(c, d, ctxs))
        copy.start()
        att_copies.append(copy)
    for copy in tab_copies:
        copy.wait_recv()
    pending += tab_copies
    for a in range(reqs):
        at = step(r, a, reqs) * ctxs
        for p in range(ctxs // 2):
            codes[a, :, p * 128 : (p + 1) * 128] = tab[at + 2 * p] + tab[at + 2 * p + 1]
    slot_at = lax.broadcasted_iota(jnp.int32, (rb, own_toks), 0).astype(F32) + 1.0

    def make_pick(e, carry):
        at = pl.ds(pl.multiple_of(e * rb, rb), rb)
        for a in range(reqs):
            mine = slot_at == codes[a, pl.ds(e, 1), :]
            gate = codes[a, pl.ds(exp_dev + e, 1), :]
            pick[a, at, :] = jnp.where(mine, 1.0, 0.0).astype(BF16)
            pickg[a, at, :] = jnp.where(mine, gate, 0.0).astype(BF16)
        return carry

    lax.fori_loop(0, exp_dev, make_pick, 0)
    loads[5].wait()
    for copy in att_copies:
        copy.wait_recv()
    pending += att_copies
    width = heads * hd
    full = dot(att[...].reshape(ctxs * block, width), ow[...], ((1,), (0,)))
    half = share // HALVES
    part_copies = []
    for p in range(HALVES):
        part[p] = full[:, p * half : (p + 1) * half].reshape(tps, block, half).astype(BF16)
        for d in range(1, tps):
            to = step(t, d, tps)
            copy = rcopy(part.at[p, to], part_recv.at[p, d], tp=to)
            copy.start()
            part_copies.append(copy)

    @pl.when(c != t)
    def _():
        res_copy.wait_recv()

    lanes = share // 128
    mine = t
    sent = []

    def relay(at, to, i, side, where, cond, p):
        copy = remote(
            tok.at[at, :, p * half : (p + 1) * half],
            tok.at[to, :, p * half : (p + 1) * half],
            tssem.at[i, side, p],
            trsem.at[to, p],
            where,
        )
        sent.append((copy, cond))
        pl.when(cond)(copy.start)

    def landed(at, cond, p):
        view = tok.at[at, :, p * half : (p + 1) * half]
        copy = remote(view, view, tssem.at[0, 0, p], trsem.at[at, p], {"tp": step(t, 1, tps)})
        pl.when(cond)(copy.wait_recv)

    def relay_far(at, i, cond, p):
        for a in range(1, reqs):
            relay(at, (reqs - a) * tps + at, i, 1 + a, {"req": step(r, a, reqs)}, cond, p)

    up_to, down_to = {"tp": jnp.minimum(t + 1, tps - 1)}, {"tp": jnp.maximum(t - 1, 0)}
    for p in range(HALVES):
        sl = slice(p * half, (p + 1) * half)
        hid = part[p, t].astype(F32) + res_t[:, sl].astype(F32)
        for d in range(1, tps):
            part_copies[p * (tps - 1) + d - 1].wait_recv()
            hid = hid + part_recv[p, d].astype(F32)
        hidden[:, sl] = hid
        for q in range(lanes // HALVES):
            q_at = p * (lanes // HALVES) + q
            tok[mine, :, q_at * 128 : (q_at + 1) * 128] = (
                hid[:, q * 128 : (q + 1) * 128] * gain_ref[pl.ds(c * lanes + q_at, 1), :]
            ).astype(BF16)
        relay(mine, mine, 0, 0, up_to, t < tps - 1, p)
        relay(mine, mine, 0, 1, down_to, t > 0, p)
        relay_far(mine, 0, t >= 0, p)
    pending += part_copies
    hid = hidden[...]
    squares = jnp.broadcast_to(jnp.sum(hid * hid, 1, keepdims=True), (block, 128))
    squares = jnp.concatenate([squares] * (128 // block), 0)
    sq[0] = jnp.transpose(squares)[0:8]
    sq_copies = []
    for d in range(1, ctxs):
        copy = rcopy(sq.at[0], sq.at[d], ctx=step(c, d, ctxs))
        copy.start()
        sq_copies.append(copy)
    for hop in range(1, tps):
        for side, from_at, inside, onward, where in (
            (0, t - hop, t >= hop, t < tps - 1, up_to),
            (1, t + hop, t < tps - hop, t > 0, down_to),
        ):
            at = jnp.clip(from_at, 0, tps - 1)
            for p in range(HALVES):
                landed(at, inside, p)
                if hop < tps - 1:
                    relay(at, at, hop, side, where, jnp.logical_and(inside, onward), p)
                relay_far(at, hop + side * (tps - 1), inside, p)
    for copy in sq_copies:
        copy.wait_recv()
    pending += sq_copies
    squares = sq[0]
    for d in range(1, ctxs):
        squares = squares + sq[d]
    fac[mine] = lax.rsqrt(squares / (share * ctxs) + 1e-6)
    for a in range(reqs):
        for d in range(tps):
            if a or d:
                there = (reqs - a) % reqs * tps + t
                copy = remote(
                    fac.at[mine],
                    fac.at[there],
                    fssem.at[a, d],
                    frsem.at[there],
                    {"req": step(r, a, reqs), "tp": step(t, d, tps)},
                )
                copy.start()
                pending.append(copy)
    for load in loads[6:8]:
        load.wait()
    n_q = quarter // rb
    first, second, third, fourth = [], [], [], []

    def up_stage(j):
        g, a = plan[j]
        x[...] = dot(
            pick[a, g * chunk : (g + 1) * chunk, :],
            tok[a * tps : (a + 1) * tps].reshape(own_toks, share),
            ((1,), (0,)),
        ).astype(BF16)

        def one(i, carry):
            e = g * members + i
            at = pl.ds(pl.multiple_of((i % n_q) * rb, rb), rb)
            xs = x[pl.ds(pl.multiple_of(i * rb, rb), rb), :]
            q = i // n_q
            gu[0, j, q // 2, q % 2, at, :] = dot(xs, wg[e], ((1,), (1,))).astype(BF16)
            gu[1, j, q // 2, q % 2, at, :] = dot(xs, wu[e], ((1,), (1,))).astype(BF16)
            return carry

        lax.fori_loop(0, members, one, 0, unroll=min(4, members))
        copy = rcopy(gu.at[:, j, :, 1 - k], r1.at[:, j], ctx=y * 2 + 1 - k)
        copy.start()
        first.append(copy)

    def pair_stage(j):
        first[j].wait_recv()
        s2[:, j] = (
            gu[:, j, 1 - y, k].astype(F32) + r1[:, j, 1 - y].astype(F32)
        ).astype(BF16)
        copy = rcopy(s2.at[:, j], r2.at[:, j], ctx=(1 - y) * 2 + k)
        copy.start()
        second.append(copy)

    def factor_rows(a):
        for d in range(tps):
            if a or d:
                at = a * tps + step(t, d, tps)
                remote(
                    fac.at[at],
                    fac.at[at],
                    fssem.at[0, 1],
                    frsem.at[at],
                    {"tp": step(t, 1, tps)},
                ).wait_recv()
        low_lane = lax.broadcasted_iota(jnp.int32, (8, 128), 1) < block
        row_at = lax.broadcasted_iota(jnp.int32, (8, 128), 0)
        for p in range(tps // 2):
            f = jnp.where(low_lane, fac[a * tps + 2 * p], fac[a * tps + 2 * p + 1])
            hi = f.astype(BF16).astype(F32)
            mid = (f - hi).astype(BF16).astype(F32)
            low = f - hi - mid
            f = jnp.where(row_at == 0, hi, jnp.where(row_at == 1, mid, low))
            frows[a, :, p * 128 : (p + 1) * 128] = jnp.where(row_at < 3, f, 0.0).astype(BF16)

    def act_stage(j):
        second[j].wait_recv()
        both = gu[:, j, y, k].astype(F32) + r1[:, j, y].astype(F32) + r2[:, j].astype(F32)
        g, a = plan[j]
        mine = pick[a, pl.ds(pl.multiple_of(g * chunk + c * quarter, quarter), quarter), :]
        row = jnp.sum(dot(mine, frows[a], ((1,), (1,))), 1, keepdims=True)
        gate = both[0] * row
        inner[j, y, k] = (gate * jax.nn.sigmoid(gate) * (both[1] * row)).astype(BF16)
        copy = rcopy(inner.at[j, y, k], inner.at[j, y, k], ctx=(1 - y) * 2 + k)
        copy.start()
        third.append(copy)

    def share_stage(j):
        third[j].wait_recv()
        copy = rcopy(inner.at[j, :, k], inner.at[j, :, k], ctx=y * 2 + 1 - k)
        copy.start()
        fourth.append(copy)

    per = tps * block
    mix_copies = []

    def down_stage(j):
        fourth[j].wait_recv()
        g, a = plan[j]

        def one(i, carry):
            e = g * members + i
            q = i // n_q
            at = pl.ds(pl.multiple_of((i % n_q) * rb, rb), rb)
            down = dot(inner[j, q // 2, q % 2, at, :], wd[e], ((1,), (0,)))
            ys[pl.ds(pl.multiple_of(i * rb, rb), rb), :] = down.astype(BF16)
            return carry

        lax.fori_loop(0, members, one, 0, unroll=min(4, members))
        term = dot(pickg[a, g * chunk : (g + 1) * chunk, :], ys[...], ((0,), (0,)))
        if g == 0:
            acc[a] = term
        else:
            acc[a] += term
        if a and g == GROUPS - 1:
            mix[a] = acc[a].astype(BF16)
            copy = rcopy(mix.at[a], mix_recv.at[a], req=step(r, a, reqs))
            copy.start()
            mix_copies.append(copy)

    stages = {"U": up_stage, "P": pair_stage, "A": act_stage, "S": share_stage, "D": down_stage}
    for line in ORDER:
        for item in line.split():
            j = int(item[1:])
            if item[0] == "U" and plan[j][1] and plan[j][0] == 0:
                for d in range(tps):
                    for p in range(HALVES):
                        landed(plan[j][1] * tps + d, t >= 0, p)
            if item[0] == "A" and plan[j][0] == 0:
                factor_rows(plan[j][1])
            if item == "D0":
                loads[8].wait()
            stages[item[0]](j)
    pending += first + second + third + fourth

    cols = share // PIECES
    pending += mix_copies
    for copy in mix_copies:
        copy.wait_recv()
    for piece in range(PIECES):
        sl = slice(piece * cols, (piece + 1) * cols)
        mixed = acc[0, :, sl]
        own = pl.ds(pl.multiple_of(t * block, block), block)
        with_hidden = acc[0, own, sl] + hidden[:, sl]
        for a in range(1, reqs):
            mixed = mixed + mix_recv[a, :, sl].astype(F32)
            with_hidden = with_hidden + mix_recv[a, own, sl].astype(F32)
        tsend[piece] = mixed.reshape(tps, block, cols).astype(BF16)
        tsend[piece, t] = with_hidden.astype(BF16)
        for d in range(1, ctxs):
            to = step(c, d, ctxs)
            copy = remote(
                tsend.at[piece, to],
                trecv.at[piece, t],
                gssem.at[piece, d],
                grsem.at[piece, t],
                {"ctx": to, "tp": c},
            )
            copy.start()
            pending.append(copy)

        @pl.when(c != t)
        def _():
            remote(
                tsend.at[piece, c],
                trecv.at[piece, t],
                gssem.at[piece, 0],
                grsem.at[piece, t],
                {"tp": c},
            ).start()

        @pl.when(c == t)
        def _():
            trecv[piece, t] = tsend[piece, c]

    for piece in range(PIECES):
        sl = slice(piece * cols, (piece + 1) * cols)

        def arrival(d):
            at = step(t, d, tps)
            return remote(
                tsend.at[piece, 0],
                trecv.at[piece, at],
                gssem.at[piece, 0],
                grsem.at[piece, at],
                {"ctx": step(c, 1, ctxs)},
            )

        @pl.when(c != t)
        def _():
            arrival(0).wait_recv()

        total = trecv[piece, t].astype(F32)
        for d in range(1, tps):
            arrival(d).wait_recv()
            total = total + trecv[piece, step(t, d, tps)].astype(F32)
        out_ref[:, sl] = total.astype(BF16)

    @pl.when(c != t)
    def _():
        res_copy.wait_send()
        for piece in range(PIECES):
            remote(
                tsend.at[piece, c],
                trecv.at[piece, t],
                gssem.at[piece, 0],
                grsem.at[piece, t],
                {"tp": c},
            ).wait_send()

    for copy, cond in sent:
        pl.when(cond)(copy.wait_send)
    for copy in pending:
        copy.wait_send()


def fused_body(
    queries,
    new_keys,
    new_values,
    cache_keys,
    cache_values,
    cache_lengths,
    residual,
    out_weight,
    norm_gain,
    expert_ids,
    gate_weights,
    w_gate,
    w_up,
    w_down,
):
    reqs, ctxs, tps = (lax.axis_size(a) for a in ("req", "ctx", "tp"))
    tok_dev, heads, hd = queries.shape
    block, share = residual.shape
    exp_dev, _, ff = w_gate.shape
    cache_dev = cache_keys.shape[1]
    blocks = reqs * ctxs
    slots = blocks * CAP
    chunks = GROUPS * reqs
    own_toks = ctxs * block
    chunk = exp_dev // GROUPS * ctxs * CAP
    quarter = chunk // ctxs
    rows = heads * block
    per, cols = tps * block, share // PIECES
    dims = (reqs, ctxs, tps, block, heads, hd, exp_dev, slots, ff, share)
    n_rem = (
        (blocks - 1)
        + 2
        + 3 * (ctxs - 1)
        + HALVES * (tps - 1)
        + (ctxs - 1)
        + 4 * chunks
        + (reqs - 1)
    )
    vmem = pl.BlockSpec(memory_space=pltpu.VMEM)
    anywhere = pl.BlockSpec(memory_space=pl.ANY)
    scratch = [
        ((exp_dev, ff, share), BF16),
        ((exp_dev, ff, share), BF16),
        ((exp_dev, ff, share), BF16),
        ((cache_dev + block, hd + 128), BF16),
        ((cache_dev, hd), BF16),
        ((block, hd), BF16),
        ((ctxs * rows, hd + 128), BF16),
        ((heads * hd, share), BF16),
        ((reqs, 2 * exp_dev, 128), F32),
        ((ctxs, hd, rows), BF16),
        ((ctxs, hd, rows), BF16),
        ((ctxs, 8, rows), F32),
        ((ctxs, 8, rows), F32),
        ((rows, hd), F32),
        ((ctxs, block, heads * hd), BF16),
        ((HALVES, tps, block, share // HALVES), BF16),
        ((HALVES, tps, block, share // HALVES), BF16),
        ((block, share), BF16),
        ((block, share), F32),
        ((ctxs, 8, 128), F32),
        ((reqs * tps, 8, 128), F32),
        ((reqs, 8, own_toks), BF16),
        ((blocks, 2 * exp_dev, 128), F32),
        ((reqs, 2 * exp_dev, own_toks), F32),
        ((reqs * tps, block, share), BF16),
        ((reqs, exp_dev * ctxs * CAP, own_toks), BF16),
        ((reqs, exp_dev * ctxs * CAP, own_toks), BF16),
        ((chunk, share), BF16),
        ((2, chunks, 2, 2, quarter, ff), BF16),
        ((2, chunks, 2, quarter, ff), BF16),
        ((2, chunks, quarter, ff), BF16),
        ((2, chunks, quarter, ff), BF16),
        ((chunks, 2, 2, quarter, ff), BF16),
        ((chunk, share), BF16),
        ((reqs, own_toks, share), F32),
        ((reqs, per, share), BF16),
        ((reqs, per, share), BF16),
        ((PIECES, tps, block, cols), BF16),
        ((PIECES, tps, block, cols), BF16),
    ]
    return pl.pallas_call(
        functools.partial(layer_kernel, dims),
        out_shape=jax.ShapeDtypeStruct((block, share), BF16),
        in_specs=[pl.BlockSpec(memory_space=pltpu.SMEM)] + [vmem] * 4 + [anywhere] * 9,
        out_specs=vmem,
        scratch_shapes=[pltpu.VMEM(*s) for s in scratch]
        + [
            pltpu.SemaphoreType.DMA((9,)),
            pltpu.SemaphoreType.DMA((n_rem,)),
            pltpu.SemaphoreType.DMA((n_rem,)),
            pltpu.SemaphoreType.DMA((PIECES, ctxs)),
            pltpu.SemaphoreType.DMA((PIECES, tps)),
            pltpu.SemaphoreType.DMA((2 * tps - 1, reqs + 1, HALVES)),
            pltpu.SemaphoreType.DMA((reqs * tps, HALVES)),
            pltpu.SemaphoreType.DMA((reqs, tps)),
            pltpu.SemaphoreType.DMA((reqs * tps,)),
        ],
        compiler_params=pltpu.CompilerParams(
            collective_id=0, has_side_effects=True, vmem_limit_bytes=63 * 1024 * 1024
        ),
    )(
        cache_lengths,
        expert_ids.T,
        gate_weights.T,
        norm_gain.reshape(-1, 128),
        residual,
        queries.reshape(tok_dev * heads, hd),
        cache_keys[0, :, 0, :],
        cache_values[0, :, 0, :],
        new_keys[:, 0, :],
        new_values[:, 0, :],
        out_weight,
        jnp.swapaxes(w_gate, 1, 2),
        jnp.swapaxes(w_up, 1, 2),
        w_down,
    )


def attention_part(queries, new_keys, new_values, cache_keys, cache_values, length):
    ctx_pos, ctx_count = lax.axis_index("ctx"), lax.axis_size("ctx")
    tok_dev, heads, hd = queries.shape
    cache_dev = cache_keys.shape[1]
    block = tok_dev // ctx_count
    rows = heads * block
    q = queries.reshape(ctx_count, block, heads, hd).transpose(0, 2, 1, 3)
    q = q.reshape(ctx_count * rows, hd)
    keys = jnp.concatenate([cache_keys[0, :, 0, :], new_keys[:, 0, :]], 0)
    values = jnp.concatenate([cache_values[0, :, 0, :], new_values[:, 0, :]], 0)
    scores = jnp.dot(keys, q.T, preferred_element_type=jnp.float32) * (hd**-0.5)
    key_at = jnp.arange(cache_dev + tok_dev, dtype=jnp.int32)[:, None]
    row_at = jnp.arange(ctx_count * rows, dtype=jnp.int32)[None, :]
    token = (row_at // rows) * block + row_at % block
    valid = jnp.where(
        key_at < cache_dev,
        ctx_pos * cache_dev + key_at < length,
        jnp.logical_and(ctx_pos == ctx_count - 1, key_at - cache_dev <= token),
    )
    scores = jnp.where(valid, scores, MASKED)
    top = jnp.max(scores, 0, keepdims=True)
    weights = jnp.where(valid, jnp.exp(scores - top), 0.0)
    total = jnp.sum(weights, 0, keepdims=True)
    sums = lax.dot_general(
        values,
        weights.astype(jnp.bfloat16),
        (((0,), (0,)), ((), ())),
        preferred_element_type=jnp.float32,
    )
    pack = jnp.concatenate([sums, top, total, jnp.zeros((6, ctx_count * rows), jnp.float32)], 0)
    return pack.reshape(hd + 8, ctx_count, rows).transpose(1, 0, 2)


def merge(packs, hd, heads):
    top = jnp.max(packs[:, hd : hd + 1], 0)
    factor = jnp.exp(packs[:, hd : hd + 1] - top)
    total = jnp.sum(factor * packs[:, hd + 1 : hd + 2], 0)
    out = (jnp.sum(factor * packs[:, :hd], 0) / total).astype(jnp.bfloat16)
    block = out.shape[1] // heads
    return out.reshape(hd, heads, block).transpose(2, 1, 0).reshape(block, heads * hd)


def route_tables(expert_ids, gate_weights, exp_dev):
    block = expert_ids.shape[0]
    both = jnp.concatenate([expert_ids.astype(jnp.float32), gate_weights], 1)
    both = lax.all_gather(both, ("req", "ctx"))
    blocks = both.shape[0]
    ids = both[:, :, :TOP].astype(jnp.int32)
    gates = both[:, :, TOP:]
    first = lax.axis_index("req") * exp_dev
    experts = first + jnp.arange(exp_dev, dtype=jnp.int32)
    hits = ids[:, :, :, None] == experts
    gate_at = jnp.sum(jnp.where(hits, gates[..., None], 0.0), 2)
    hit = jnp.any(hits, 2)
    earlier = jnp.tril(jnp.ones((block, block), jnp.bfloat16), -1)
    rank = jnp.einsum(
        "ij,bje->bie", earlier, hit.astype(jnp.bfloat16), preferred_element_type=jnp.float32
    )
    code = jnp.arange(blocks, dtype=jnp.int32)[:, None, None] * CAP + rank.astype(jnp.int32)
    code = jnp.where(hit, code, -1)
    flat = (blocks * block, exp_dev)
    return code.reshape(flat).T, gate_at.reshape(flat).T


def spread_body(
    queries,
    new_keys,
    new_values,
    cache_keys,
    cache_values,
    cache_lengths,
    residual,
    out_weight,
    norm_gain,
    expert_ids,
    gate_weights,
    w_gate,
    w_up,
    w_down,
):
    ctx_pos, tp_pos, req_pos = (lax.axis_index(a) for a in ("ctx", "tp", "req"))
    ctx_count, req_count = lax.axis_size("ctx"), lax.axis_size("req")
    tok_dev, heads, hd = queries.shape
    block, share = residual.shape
    exp_dev = w_gate.shape[0]
    slots = req_count * ctx_count * CAP
    length = lax.dynamic_index_in_dim(cache_lengths, req_pos, 0, keepdims=False)
    code, gate_at = route_tables(expert_ids, gate_weights, exp_dev)
    swap = [(a * ctx_count + b, b * ctx_count + a) for a in range(ctx_count) for b in range(ctx_count)]
    residual_t = lax.ppermute(residual, ("ctx", "tp"), swap)
    packs = attention_part(queries, new_keys, new_values, cache_keys, cache_values, length)
    packs = lax.all_to_all(packs, "ctx", 0, 0, tiled=True)
    attended = merge(packs, hd, heads)
    attended = lax.all_gather(attended, "ctx", tiled=True)
    part = jnp.dot(attended, out_weight, preferred_element_type=jnp.float32)
    part = part.reshape(-1, block, share)
    part = lax.all_to_all(part, "tp", 0, 0, tiled=True)
    hidden = jnp.sum(part, 0) + residual_t.astype(jnp.float32)
    squares = jnp.sum(hidden * hidden, 1)
    gain = lax.dynamic_slice_in_dim(norm_gain, ctx_pos * share, share, 0)
    scaled = (hidden * gain).astype(jnp.bfloat16)
    squares = lax.psum(squares, "ctx")
    factor = lax.rsqrt(squares / norm_gain.shape[0] + 1e-6)
    factor = lax.all_gather(factor, ("req", "tp"), tiled=True)
    scaled = lax.all_gather(scaled, ("req", "tp"), tiled=True)
    pick = code[:, None, :] == jnp.arange(slots, dtype=jnp.int32)[None, :, None]
    row_factor = jnp.sum(jnp.where(pick, factor, 0.0), -1, keepdims=True)
    row_gate = jnp.sum(jnp.where(pick, gate_at[:, None, :], 0.0), -1, keepdims=True)
    pick = pick.astype(jnp.bfloat16)
    rows = jnp.einsum("est,td->esd", pick, scaled, preferred_element_type=jnp.bfloat16)
    gate = jnp.einsum("esd,edf->esf", rows, w_gate, preferred_element_type=jnp.float32)
    up = jnp.einsum("esd,edf->esf", rows, w_up, preferred_element_type=jnp.float32)
    both = jnp.stack([gate, up], 2).astype(jnp.bfloat16)
    both = both.reshape(ctx_count, exp_dev * slots // ctx_count, 2, -1)
    both = lax.all_to_all(both, "ctx", 0, 0, tiled=True)
    both = both.astype(jnp.float32).sum(0)
    per = exp_dev * slots // ctx_count
    mine = lax.dynamic_slice_in_dim(row_factor.reshape(-1, 1), ctx_pos * per, per, 0)
    inner = (jax.nn.silu(both[:, 0] * mine) * (both[:, 1] * mine)).astype(jnp.bfloat16)
    inner = lax.all_gather(inner, "ctx", tiled=True).reshape(exp_dev, slots, -1)
    down = jnp.einsum("esf,efd->esd", inner, w_down, preferred_element_type=jnp.float32)
    down = (down * row_gate).astype(jnp.bfloat16)
    mixed = jnp.einsum("est,esd->td", pick, down, preferred_element_type=jnp.float32)
    mixed = mixed.astype(jnp.bfloat16).reshape(-1, block, share)
    mixed = lax.all_to_all(mixed, ("req", "tp"), 0, 0, tiled=True)
    out = hidden + jnp.sum(mixed.astype(jnp.float32), 0)
    return lax.ppermute(out.astype(jnp.bfloat16), ("ctx", "tp"), swap)


def body(*args):
    tokens = args[0].shape[0] * lax.axis_size("req")
    slots = args[11].shape[0] * lax.axis_size("req") * lax.axis_size("ctx") * CAP
    if tokens * slots * 2 <= FUSED_BYTES:
        return fused_body(*args)
    return spread_body(*args)


def solution(mesh):
    in_specs = (
        P("req", "tp", None),
        P("req", "tp", None),
        P("req", "tp", None),
        P("req", "ctx", "tp", None),
        P("req", "ctx", "tp", None),
        P(),
        P(("req", "ctx"), "tp"),
        P("tp", "ctx"),
        P(),
        P(("req", "ctx"), None),
        P(("req", "ctx"), None),
        P("req", "ctx", "tp"),
        P("req", "ctx", "tp"),
        P("req", "tp", "ctx"),
    )
    out_specs = P(("req", "ctx"), "tp")
    return jax.shard_map(body, mesh=mesh, in_specs=in_specs, out_specs=out_specs, check_vma=False)
```

```python
import functools
import jax
import jax.numpy as jnp
from jax import lax
from jax.experimental import pallas as pl
from jax.experimental.pallas import tpu as pltpu
from jax.sharding import PartitionSpec as P

TOP = 6
CAP = 8
MASKED = -1e30
F32 = jnp.float32
BF16 = jnp.bfloat16
GROUPS = 4
PIECES = 2
HALVES = 2
ORDER = (
    "U0 P0 U1 W1",
    "P1 W2 P2 A0",
    "W3 P3 P4 A1",
    "A2 A3 S0 S1",
    "A4 P5 P6 P7",
    "S2 S3 D0 D1",
    "S4 D2 D3 D4",
    "A5 A6 A7 S5",
    "S6 D5 S7 D6",
    "D7",
)
FUSED_BYTES = 4 * 1024 * 1024


def dot(a, b, contract, kind=F32):
    return lax.dot_general(a, b, (contract, ((), ())), preferred_element_type=kind)


def layer_kernel(
    dims,
    len_ref,
    ids_ref,
    gw_ref,
    gain_ref,
    res_ref,
    q_hbm,
    ck_hbm,
    cv_hbm,
    nk_hbm,
    nv_hbm,
    ow_hbm,
    wg_hbm,
    wu_hbm,
    wd_hbm,
    out_ref,
    wg,
    wu,
    wd,
    keys,
    vals,
    nvals,
    qa,
    ow,
    rt,
    pk_send,
    pk_recv,
    st_send,
    st_recv,
    turned,
    att,
    part,
    part_recv,
    res_t,
    hidden,
    sq,
    fac,
    frows,
    tab,
    codes,
    tok,
    pick,
    pickg,
    x,
    gu,
    r1,
    s2,
    r2,
    p1,
    p2,
    inner,
    ys,
    acc,
    mix,
    mix_recv,
    tsend,
    trecv,
    w_sem,
    ssem,
    rsem,
    gssem,
    grsem,
    tssem,
    trsem,
    fssem,
    frsem,
):
    reqs, ctxs, tps, block, heads, hd, exp_dev, slots, ff, share = dims
    r, c, t = lax.axis_index("req"), lax.axis_index("ctx"), lax.axis_index("tp")
    blocks = reqs * ctxs
    own_toks = ctxs * block
    rb = ctxs * CAP
    members = exp_dev // GROUPS
    chunk = members * rb
    quarter = chunk // ctxs
    plan = (
        [(0, 0)]
        + [(g, a) for a in range(1, reqs) for g in range(GROUPS)]
        + [(g, 0) for g in range(1, GROUPS)]
    )
    y, k = c // 2, c % 2
    count = [0]

    def remote(src, dst, send, recv, where):
        return pltpu.make_async_remote_copy(
            src_ref=src,
            dst_ref=dst,
            send_sem=send,
            recv_sem=recv,
            device_id={"req": r, "ctx": c, "tp": t} | where,
            device_id_type=pl.DeviceIdType.MESH,
        )

    def rcopy(src, dst, **where):
        i = count[0]
        count[0] = i + 1
        return remote(src, dst, ssem.at[i], rsem.at[i], where)

    def step(me, d, n):
        return lax.rem(me + d, n)

    cache_dev = ck_hbm.shape[0]
    rows = heads * block
    fresh = pl.ds(pl.multiple_of(c * block, block), block)
    loads = [
        pltpu.make_async_copy(src, dst, w_sem.at[i])
        for i, (src, dst) in enumerate(
            [
                (q_hbm, qa.at[:, 0:hd]),
                (ck_hbm, keys.at[0:cache_dev, 0:hd]),
                (nk_hbm.at[fresh], keys.at[cache_dev : cache_dev + block, 0:hd]),
                (cv_hbm, vals),
                (nv_hbm.at[fresh], nvals),
                (ow_hbm, ow),
                (wg_hbm, wg),
                (wu_hbm, wu),
                (wd_hbm, wd),
            ]
        )
    ]
    for load in loads[:6]:
        load.start()

    barrier = pltpu.get_barrier_semaphore()
    peers = [
        {"req": step(r, a, reqs), "ctx": step(c, b, ctxs), "tp": t}
        for a in range(reqs)
        for b in range(ctxs)
        if a or b
    ] + [
        {"req": step(r, a, reqs), "ctx": c, "tp": step(t, d, tps)}
        for a in range(reqs)
        for d in range(1, tps)
    ]
    swap = {"ctx": t, "tp": c}
    across = [{"req": r, "ctx": step(c, d, ctxs), "tp": c} for d in range(1, ctxs)] + [
        {"req": r, "ctx": t, "tp": step(t, d, tps)} for d in range(1, tps)
    ]

    def greet(peer):
        pl.semaphore_signal(barrier, 1, device_id=peer, device_id_type=pl.DeviceIdType.MESH)

    for peer in peers:
        greet(peer)

    @pl.when(c != t)
    def _():
        for peer in across:
            greet(peer)
        pl.semaphore_wait(barrier, len(peers) + len(across))

    @pl.when(c == t)
    def _():
        pl.semaphore_wait(barrier, len(peers))

    pending = []

    me = r * ctxs + c
    res_copy = rcopy(res_ref, res_t, **swap)

    @pl.when(c != t)
    def _():
        res_copy.start()

    @pl.when(c == t)
    def _():
        res_t[...] = res_ref[...]

    length = len_ref[r]
    scale = hd**-0.5
    lean = scale * 1.4426950408889634
    wide = keys.shape[1]
    old_at = lax.broadcasted_iota(jnp.int32, (cache_dev, wide - hd), 0)
    lane_at = lax.broadcasted_iota(jnp.int32, (cache_dev, wide - hd), 1)
    hide = jnp.logical_and(old_at >= length - c * cache_dev, lane_at == 0)
    keys[0:cache_dev, hd:wide] = jnp.where(hide, MASKED, 0.0).astype(BF16)
    qa[:, hd:wide] = jnp.ones((ctxs * rows, wide - hd), BF16)
    new_at = lax.broadcasted_iota(jnp.int32, (block, rows), 0) + c * block
    tok_at = lax.broadcasted_iota(jnp.int32, (block, rows), 1) // heads
    stat_at = lax.broadcasted_iota(jnp.int32, (8, rows), 0)
    for load in loads[:5]:
        load.wait()
    for load in loads[6:]:
        load.start()
    tile = cache_dev // 4
    pk_copies = []
    tab_copies = []
    for d in list(range(1, ctxs)) + [0]:
        b = step(c, d, ctxs)
        at = pl.ds(pl.multiple_of(b * rows, rows), rows)
        scores = [
            dot(keys[i : i + tile, :], qa[at, :], ((1,), (1,))) for i in range(0, cache_dev, tile)
        ]
        new = dot(keys[cache_dev : cache_dev + block, 0:hd], qa[at, 0:hd], ((1,), (1,)))
        scores.append(jnp.where(new_at <= tok_at + b * block, new, MASKED))
        tops = [jnp.max(s, 0, keepdims=True) for s in scores]
        top = jnp.maximum(functools.reduce(jnp.maximum, tops), -1e28)
        total, sums = None, None
        for i, s in enumerate(scores):
            w = jnp.exp2((s - top) * lean)
            v = vals[i * tile : (i + 1) * tile, :] if i * tile < cache_dev else nvals[...]
            part_total = jnp.sum(w, 0, keepdims=True)
            part_sums = dot(v, w.astype(BF16), ((0,), (0,)))
            total = part_total if total is None else total + part_total
            sums = part_sums if sums is None else sums + part_sums
        pk_send[d] = sums.astype(BF16)
        st_send[d] = jnp.where(
            stat_at == 0, top * scale, jnp.where(stat_at == 1, total, 0.0)
        )
        if d:
            for src, dst in ((pk_send, pk_recv), (st_send, st_recv)):
                copy = rcopy(src.at[d], dst.at[d], ctx=b)
                copy.start()
                pk_copies.append(copy)
        if d == 1:
            n_exp = reqs * exp_dev
            ids = jnp.concatenate([ids_ref[...]] * (128 // block), 1)
            gws = jnp.concatenate([gw_ref[...]] * (128 // block), 1)
            half = lax.broadcasted_iota(jnp.int32, ids.shape, 1) // block
            ids = jnp.where(half == lax.rem(me, 128 // block), ids, -1)
            exp_at = lax.broadcasted_iota(jnp.int32, (n_exp, 128), 0)
            hit = jnp.zeros((n_exp, 128), F32)
            gates = jnp.zeros((n_exp, 128), F32)
            for route in range(TOP):
                same = ids[route : route + 1, :] == exp_at
                hit = hit + jnp.where(same, 1.0, 0.0)
                gates = gates + jnp.where(same, gws[route : route + 1, :], 0.0)
            one_at = lax.broadcasted_iota(jnp.int32, (128, 128), 0)
            two_at = lax.broadcasted_iota(jnp.int32, (128, 128), 1)
            upto = jnp.where(one_at <= two_at, 1.0, 0.0).astype(BF16)
            rank = dot(hit.astype(BF16), upto, ((1,), (0,)))
            code = jnp.where(hit > 0.0, rank + (c * CAP).astype(F32), 0.0)
            for a in range(reqs):
                rt[a, 0:exp_dev, :] = code[a * exp_dev : (a + 1) * exp_dev]
                rt[a, exp_dev : 2 * exp_dev, :] = gates[a * exp_dev : (a + 1) * exp_dev]
            for a in range(reqs):
                for b2 in range(ctxs):
                    if a or b2:
                        to = step(r, a, reqs)
                        copy = rcopy(rt.at[to], tab.at[me], req=to, ctx=step(c, b2, ctxs))
                        copy.start()
                        tab_copies.append(copy)
            tab[me] = rt[r]
    for copy in pk_copies:
        copy.wait_recv()
    pending += pk_copies
    packs = [pk_send[0]] + [pk_recv[d] for d in range(1, ctxs)]
    stats = [st_send[0]] + [st_recv[d] for d in range(1, ctxs)]
    tops = [st[0:1, :] for st in stats]
    top = functools.reduce(jnp.maximum, tops)
    total = jnp.zeros((1, rows), F32)
    sums = jnp.zeros((hd, rows), F32)
    for p, st, own in zip(packs, stats, tops):
        factor = jnp.exp(own - top)
        total = total + factor * st[1:2, :]
        sums = sums + factor * p.astype(F32)
    turned[...] = jnp.transpose(sums / total)
    for h in range(heads):
        att[c, :, h * hd : (h + 1) * hd] = turned[pl.ds(h, block, stride=heads), :].astype(BF16)
    att_copies = []
    for d in range(1, ctxs):
        copy = rcopy(att.at[c], att.at[c], ctx=step(c, d, ctxs))
        copy.start()
        att_copies.append(copy)
    for copy in tab_copies:
        copy.wait_recv()
    pending += tab_copies
    for a in range(reqs):
        at = step(r, a, reqs) * ctxs
        for p in range(ctxs // 2):
            codes[a, :, p * 128 : (p + 1) * 128] = tab[at + 2 * p] + tab[at + 2 * p + 1]
    slot_at = lax.broadcasted_iota(jnp.int32, (rb, own_toks), 0).astype(F32) + 1.0

    def make_pick(e, carry):
        at = pl.ds(pl.multiple_of(e * rb, rb), rb)
        for a in range(reqs):
            mine = slot_at == codes[a, pl.ds(e, 1), :]
            gate = codes[a, pl.ds(exp_dev + e, 1), :]
            pick[a, at, :] = jnp.where(mine, 1.0, 0.0).astype(BF16)
            pickg[a, at, :] = jnp.where(mine, gate, 0.0).astype(BF16)
        return carry

    lax.fori_loop(0, exp_dev, make_pick, 0)
    loads[5].wait()
    for copy in att_copies:
        copy.wait_recv()
    pending += att_copies
    width = heads * hd
    full = dot(att[...].reshape(ctxs * block, width), ow[...], ((1,), (0,)))
    half = share // HALVES
    part_copies = []
    for p in range(HALVES):
        part[p] = full[:, p * half : (p + 1) * half].reshape(tps, block, half).astype(BF16)
        for d in range(1, tps):
            to = step(t, d, tps)
            copy = rcopy(part.at[p, to], part_recv.at[p, d], tp=to)
            copy.start()
            part_copies.append(copy)

    @pl.when(c != t)
    def _():
        res_copy.wait_recv()

    lanes = share // 128
    mine = t
    sent = []

    def relay(at, to, i, side, where, cond, p):
        copy = remote(
            tok.at[at, :, p * half : (p + 1) * half],
            tok.at[to, :, p * half : (p + 1) * half],
            tssem.at[i, side, p],
            trsem.at[to, p],
            where,
        )
        sent.append((copy, cond))
        pl.when(cond)(copy.start)

    def landed(at, cond, p):
        view = tok.at[at, :, p * half : (p + 1) * half]
        copy = remote(view, view, tssem.at[0, 0, p], trsem.at[at, p], {"tp": step(t, 1, tps)})
        pl.when(cond)(copy.wait_recv)

    def relay_far(at, i, cond, p):
        for a in range(1, reqs):
            relay(at, (reqs - a) * tps + at, i, 1 + a, {"req": step(r, a, reqs)}, cond, p)

    up_to, down_to = {"tp": jnp.minimum(t + 1, tps - 1)}, {"tp": jnp.maximum(t - 1, 0)}
    for p in range(HALVES):
        sl = slice(p * half, (p + 1) * half)
        hid = part[p, t].astype(F32) + res_t[:, sl].astype(F32)
        for d in range(1, tps):
            part_copies[p * (tps - 1) + d - 1].wait_recv()
            hid = hid + part_recv[p, d].astype(F32)
        hidden[:, sl] = hid
        for q in range(lanes // HALVES):
            q_at = p * (lanes // HALVES) + q
            tok[mine, :, q_at * 128 : (q_at + 1) * 128] = (
                hid[:, q * 128 : (q + 1) * 128] * gain_ref[pl.ds(c * lanes + q_at, 1), :]
            ).astype(BF16)
        relay(mine, mine, 0, 0, up_to, t < tps - 1, p)
        relay(mine, mine, 0, 1, down_to, t > 0, p)
        relay_far(mine, 0, t >= 0, p)
    pending += part_copies
    hid = hidden[...]
    squares = jnp.broadcast_to(jnp.sum(hid * hid, 1, keepdims=True), (block, 128))
    squares = jnp.concatenate([squares] * (128 // block), 0)
    sq[0] = jnp.transpose(squares)[0:8]
    sq_copies = []
    for d in range(1, ctxs):
        copy = rcopy(sq.at[0], sq.at[d], ctx=step(c, d, ctxs))
        copy.start()
        sq_copies.append(copy)
    for hop in range(1, tps):
        for p in range(HALVES):
            for side, from_at, inside, onward, where in (
                (0, t - hop, t >= hop, t < tps - 1, up_to),
                (1, t + hop, t < tps - hop, t > 0, down_to),
            ):
                at = jnp.clip(from_at, 0, tps - 1)
                landed(at, inside, p)
                if hop < tps - 1:
                    relay(at, at, hop, side, where, jnp.logical_and(inside, onward), p)
                relay_far(at, hop + side * (tps - 1), inside, p)
    for copy in sq_copies:
        copy.wait_recv()
    pending += sq_copies
    squares = sq[0]
    for d in range(1, ctxs):
        squares = squares + sq[d]
    fac[mine] = lax.rsqrt(squares / (share * ctxs) + 1e-6)
    for a in range(reqs):
        for d in range(tps):
            if a or d:
                there = (reqs - a) % reqs * tps + t
                copy = remote(
                    fac.at[mine],
                    fac.at[there],
                    fssem.at[a, d],
                    frsem.at[there],
                    {"req": step(r, a, reqs), "tp": step(t, d, tps)},
                )
                copy.start()
                pending.append(copy)
    for load in loads[6:8]:
        load.wait()
    n_q = quarter // rb
    first, second, third, fourth = {}, [], [], []

    def up_stage(*js):
        g = plan[js[0]][0]
        for j in js:
            a = plan[j][1]
            x[a] = dot(
                pick[a, g * chunk : (g + 1) * chunk, :],
                tok[a * tps : (a + 1) * tps].reshape(own_toks, share),
                ((1,), (0,)),
            ).astype(BF16)

        def one(i, carry):
            e = g * members + i
            at = pl.ds(pl.multiple_of((i % n_q) * rb, rb), rb)
            from_at = pl.ds(pl.multiple_of(i * rb, rb), rb)
            xs = jnp.concatenate([x[plan[j][1], from_at, :] for j in js], 0)
            q = i // n_q
            for w, weight in enumerate((wg, wu)):
                res = dot(xs, weight[e], ((1,), (1,))).astype(BF16)
                for m, j in enumerate(js):
                    gu[w, j, q // 2, q % 2, at, :] = res[m * rb : (m + 1) * rb]
            return carry

        lax.fori_loop(0, members, one, 0, unroll=min(4, members))
        for j in js:
            copy = rcopy(gu.at[:, j, :, 1 - k], r1.at[:, j], ctx=y * 2 + 1 - k)
            copy.start()
            first[j] = copy

    def both_stage(g):
        up_stage(*[j for j in range(len(plan)) if plan[j][0] == g])

    whole = ff // 128 * 128

    def pack(ref, j, arrays, cuts):
        at = 0
        for v in arrays:
            for m in range(0, whole, 128):
                ref[j, at : at + quarter, :] = v[:, m : m + 128].astype(BF16)
                at += quarter
        n = quarter // cuts
        ends = jnp.concatenate(
            [v[i * n : (i + 1) * n, whole:ff] for v in arrays for i in range(cuts)], 1
        )
        for m in range(0, ends.shape[1], 128):
            ref[j, at : at + n, :] = ends[:, m : m + 128].astype(BF16)
            at += n

    def unpack(ref, j, count_of, cuts):
        at = 0
        mains = []
        for _ in range(count_of):
            tiles = []
            for _ in range(0, whole, 128):
                tiles.append(ref[j, at : at + quarter, :].astype(F32))
                at += quarter
            mains.append(tiles)
        n, rest = quarter // cuts, ff - whole
        ends = []
        for _ in range(0, count_of * cuts * rest, 128):
            ends.append(ref[j, at : at + n, :].astype(F32))
            at += n
        ends = jnp.concatenate(ends, 1)
        out = []
        for v in range(count_of):
            last = [
                ends[:, i * rest : (i + 1) * rest] for i in range(v * cuts, (v + 1) * cuts)
            ]
            out.append(jnp.concatenate(mains[v] + [jnp.concatenate(last, 0)], 1))
        return out

    def pair_stage(j):
        first[j].wait_recv()
        both = gu[:, j, 1 - y, k].astype(F32) + r1[:, j, 1 - y].astype(F32)
        pack(s2, j, [both[0], both[1]], 2)
        copy = rcopy(s2.at[j], r2.at[j], ctx=(1 - y) * 2 + k)
        copy.start()
        second.append(copy)

    def factor_rows(a):
        for d in range(tps):
            if a or d:
                at = a * tps + step(t, d, tps)
                remote(
                    fac.at[at],
                    fac.at[at],
                    fssem.at[0, 1],
                    frsem.at[at],
                    {"tp": step(t, 1, tps)},
                ).wait_recv()
        low_lane = lax.broadcasted_iota(jnp.int32, (8, 128), 1) < block
        row_at = lax.broadcasted_iota(jnp.int32, (8, 128), 0)
        for p in range(tps // 2):
            f = jnp.where(low_lane, fac[a * tps + 2 * p], fac[a * tps + 2 * p + 1])
            hi = f.astype(BF16).astype(F32)
            mid = (f - hi).astype(BF16).astype(F32)
            low = f - hi - mid
            f = jnp.where(row_at == 0, hi, jnp.where(row_at == 1, mid, low))
            frows[a, :, p * 128 : (p + 1) * 128] = jnp.where(row_at < 3, f, 0.0).astype(BF16)

    def act_stage(j):
        second[j].wait_recv()
        both = gu[:, j, y, k].astype(F32) + r1[:, j, y].astype(F32)
        other = unpack(r2, j, 2, 2)
        g, a = plan[j]
        mine = pick[a, pl.ds(pl.multiple_of(g * chunk + c * quarter, quarter), quarter), :]
        row = jnp.sum(dot(mine, frows[a], ((1,), (1,))), 1, keepdims=True)
        gate = (both[0] + other[0]) * row
        act = gate * jax.nn.sigmoid(gate) * ((both[1] + other[1]) * row)
        pack(p1, j, [act], 4)
        copy = rcopy(p1.at[j], p2.at[j], ctx=(1 - y) * 2 + k)
        copy.start()
        third.append(copy)
        inner[j, y, k] = act.astype(BF16)

    def share_stage(j):
        third[j].wait_recv()
        inner[j, 1 - y, k] = unpack(p2, j, 1, 4)[0].astype(BF16)
        copy = rcopy(inner.at[j, :, k], inner.at[j, :, k], ctx=y * 2 + 1 - k)
        copy.start()
        fourth.append(copy)

    per = tps * block
    mix_copies = []

    def down_stage(j):
        fourth[j].wait_recv()
        g, a = plan[j]

        def one(i, carry):
            e = g * members + i
            q = i // n_q
            at = pl.ds(pl.multiple_of((i % n_q) * rb, rb), rb)
            down = dot(inner[j, q // 2, q % 2, at, :], wd[e], ((1,), (0,)))
            ys[pl.ds(pl.multiple_of(i * rb, rb), rb), :] = down.astype(BF16)
            return carry

        lax.fori_loop(0, members, one, 0, unroll=min(4, members))
        term = dot(pickg[a, g * chunk : (g + 1) * chunk, :], ys[...], ((0,), (0,)))
        if g == 0:
            acc[a] = term
        else:
            acc[a] += term
        if a and g == GROUPS - 1:
            mix[a] = acc[a].astype(BF16)
            copy = rcopy(mix.at[a], mix_recv.at[a], req=step(r, a, reqs))
            copy.start()
            mix_copies.append(copy)

    stages = {"U": up_stage, "W": both_stage, "P": pair_stage, "A": act_stage, "S": share_stage, "D": down_stage}
    for line in ORDER:
        for item in line.split():
            j = int(item[1:])
            if item[0] == "U" and plan[j][1] and plan[j][0] == 0:
                for d in range(tps):
                    for p in range(HALVES):
                        landed(plan[j][1] * tps + d, t >= 0, p)
            if item[0] == "A" and plan[j][0] == 0:
                factor_rows(plan[j][1])
            if item == "D0":
                loads[8].wait()
            stages[item[0]](j)
    pending += list(first.values()) + second + third + fourth

    cols = share // PIECES
    pending += mix_copies
    for copy in mix_copies:
        copy.wait_recv()
    for piece in range(PIECES):
        sl = slice(piece * cols, (piece + 1) * cols)
        mixed = acc[0, :, sl]
        own = pl.ds(pl.multiple_of(t * block, block), block)
        with_hidden = acc[0, own, sl] + hidden[:, sl]
        for a in range(1, reqs):
            mixed = mixed + mix_recv[a, :, sl].astype(F32)
            with_hidden = with_hidden + mix_recv[a, own, sl].astype(F32)
        tsend[piece] = mixed.reshape(tps, block, cols).astype(BF16)
        tsend[piece, t] = with_hidden.astype(BF16)
        for d in range(1, ctxs):
            to = step(c, d, ctxs)
            copy = remote(
                tsend.at[piece, to],
                trecv.at[piece, t],
                gssem.at[piece, d],
                grsem.at[piece, t],
                {"ctx": to, "tp": c},
            )
            copy.start()
            pending.append(copy)

        @pl.when(c != t)
        def _():
            remote(
                tsend.at[piece, c],
                trecv.at[piece, t],
                gssem.at[piece, 0],
                grsem.at[piece, t],
                {"tp": c},
            ).start()

        @pl.when(c == t)
        def _():
            trecv[piece, t] = tsend[piece, c]

    for piece in range(PIECES):
        sl = slice(piece * cols, (piece + 1) * cols)

        def arrival(d):
            at = step(t, d, tps)
            return remote(
                tsend.at[piece, 0],
                trecv.at[piece, at],
                gssem.at[piece, 0],
                grsem.at[piece, at],
                {"ctx": step(c, 1, ctxs)},
            )

        @pl.when(c != t)
        def _():
            arrival(0).wait_recv()

        total = trecv[piece, t].astype(F32)
        for d in range(1, tps):
            arrival(d).wait_recv()
            total = total + trecv[piece, step(t, d, tps)].astype(F32)
        out_ref[:, sl] = total.astype(BF16)

    @pl.when(c != t)
    def _():
        res_copy.wait_send()
        for piece in range(PIECES):
            remote(
                tsend.at[piece, c],
                trecv.at[piece, t],
                gssem.at[piece, 0],
                grsem.at[piece, t],
                {"tp": c},
            ).wait_send()

    for copy, cond in sent:
        pl.when(cond)(copy.wait_send)
    for copy in pending:
        copy.wait_send()


def fused_body(
    queries,
    new_keys,
    new_values,
    cache_keys,
    cache_values,
    cache_lengths,
    residual,
    out_weight,
    norm_gain,
    expert_ids,
    gate_weights,
    w_gate,
    w_up,
    w_down,
):
    reqs, ctxs, tps = (lax.axis_size(a) for a in ("req", "ctx", "tp"))
    tok_dev, heads, hd = queries.shape
    block, share = residual.shape
    exp_dev, _, ff = w_gate.shape
    cache_dev = cache_keys.shape[1]
    blocks = reqs * ctxs
    slots = blocks * CAP
    chunks = GROUPS * reqs
    own_toks = ctxs * block
    chunk = exp_dev // GROUPS * ctxs * CAP
    quarter = chunk // ctxs
    rows = heads * block
    per, cols = tps * block, share // PIECES
    pair_rows = 2 * quarter * ff // 128
    dims = (reqs, ctxs, tps, block, heads, hd, exp_dev, slots, ff, share)
    n_rem = (
        (blocks - 1)
        + 2
        + 3 * (ctxs - 1)
        + HALVES * (tps - 1)
        + (ctxs - 1)
        + 4 * chunks
        + (reqs - 1)
    )
    vmem = pl.BlockSpec(memory_space=pltpu.VMEM)
    anywhere = pl.BlockSpec(memory_space=pl.ANY)
    scratch = [
        ((exp_dev, ff, share), BF16),
        ((exp_dev, ff, share), BF16),
        ((exp_dev, ff, share), BF16),
        ((cache_dev + block, hd + 128), BF16),
        ((cache_dev, hd), BF16),
        ((block, hd), BF16),
        ((ctxs * rows, hd + 128), BF16),
        ((heads * hd, share), BF16),
        ((reqs, 2 * exp_dev, 128), F32),
        ((ctxs, hd, rows), BF16),
        ((ctxs, hd, rows), BF16),
        ((ctxs, 8, rows), F32),
        ((ctxs, 8, rows), F32),
        ((rows, hd), F32),
        ((ctxs, block, heads * hd), BF16),
        ((HALVES, tps, block, share // HALVES), BF16),
        ((HALVES, tps, block, share // HALVES), BF16),
        ((block, share), BF16),
        ((block, share), F32),
        ((ctxs, 8, 128), F32),
        ((reqs * tps, 8, 128), F32),
        ((reqs, 8, own_toks), BF16),
        ((blocks, 2 * exp_dev, 128), F32),
        ((reqs, 2 * exp_dev, own_toks), F32),
        ((reqs * tps, block, share), BF16),
        ((reqs, exp_dev * ctxs * CAP, own_toks), BF16),
        ((reqs, exp_dev * ctxs * CAP, own_toks), BF16),
        ((reqs, chunk, share), BF16),
        ((2, chunks, 2, 2, quarter, ff), BF16),
        ((2, chunks, 2, quarter, ff), BF16),
        ((chunks, pair_rows, 128), BF16),
        ((chunks, pair_rows, 128), BF16),
        ((chunks, pair_rows // 2, 128), BF16),
        ((chunks, pair_rows // 2, 128), BF16),
        ((chunks, 2, 2, quarter, ff), BF16),
        ((chunk, share), BF16),
        ((reqs, own_toks, share), F32),
        ((reqs, per, share), BF16),
        ((reqs, per, share), BF16),
        ((PIECES, tps, block, cols), BF16),
        ((PIECES, tps, block, cols), BF16),
    ]
    return pl.pallas_call(
        functools.partial(layer_kernel, dims),
        out_shape=jax.ShapeDtypeStruct((block, share), BF16),
        in_specs=[pl.BlockSpec(memory_space=pltpu.SMEM)] + [vmem] * 4 + [anywhere] * 9,
        out_specs=vmem,
        scratch_shapes=[pltpu.VMEM(*s) for s in scratch]
        + [
            pltpu.SemaphoreType.DMA((9,)),
            pltpu.SemaphoreType.DMA((n_rem,)),
            pltpu.SemaphoreType.DMA((n_rem,)),
            pltpu.SemaphoreType.DMA((PIECES, ctxs)),
            pltpu.SemaphoreType.DMA((PIECES, tps)),
            pltpu.SemaphoreType.DMA((2 * tps - 1, reqs + 1, HALVES)),
            pltpu.SemaphoreType.DMA((reqs * tps, HALVES)),
            pltpu.SemaphoreType.DMA((reqs, tps)),
            pltpu.SemaphoreType.DMA((reqs * tps,)),
        ],
        compiler_params=pltpu.CompilerParams(
            collective_id=0, has_side_effects=True, vmem_limit_bytes=63 * 1024 * 1024
        ),
    )(
        cache_lengths,
        expert_ids.T,
        gate_weights.T,
        norm_gain.reshape(-1, 128),
        residual,
        queries.reshape(tok_dev * heads, hd),
        cache_keys[0, :, 0, :],
        cache_values[0, :, 0, :],
        new_keys[:, 0, :],
        new_values[:, 0, :],
        out_weight,
        jnp.swapaxes(w_gate, 1, 2),
        jnp.swapaxes(w_up, 1, 2),
        w_down,
    )


def attention_part(queries, new_keys, new_values, cache_keys, cache_values, length):
    ctx_pos, ctx_count = lax.axis_index("ctx"), lax.axis_size("ctx")
    tok_dev, heads, hd = queries.shape
    cache_dev = cache_keys.shape[1]
    block = tok_dev // ctx_count
    rows = heads * block
    q = queries.reshape(ctx_count, block, heads, hd).transpose(0, 2, 1, 3)
    q = q.reshape(ctx_count * rows, hd)
    keys = jnp.concatenate([cache_keys[0, :, 0, :], new_keys[:, 0, :]], 0)
    values = jnp.concatenate([cache_values[0, :, 0, :], new_values[:, 0, :]], 0)
    scores = jnp.dot(keys, q.T, preferred_element_type=jnp.float32) * (hd**-0.5)
    key_at = jnp.arange(cache_dev + tok_dev, dtype=jnp.int32)[:, None]
    row_at = jnp.arange(ctx_count * rows, dtype=jnp.int32)[None, :]
    token = (row_at // rows) * block + row_at % block
    valid = jnp.where(
        key_at < cache_dev,
        ctx_pos * cache_dev + key_at < length,
        jnp.logical_and(ctx_pos == ctx_count - 1, key_at - cache_dev <= token),
    )
    scores = jnp.where(valid, scores, MASKED)
    top = jnp.max(scores, 0, keepdims=True)
    weights = jnp.where(valid, jnp.exp(scores - top), 0.0)
    total = jnp.sum(weights, 0, keepdims=True)
    sums = lax.dot_general(
        values,
        weights.astype(jnp.bfloat16),
        (((0,), (0,)), ((), ())),
        preferred_element_type=jnp.float32,
    )
    pack = jnp.concatenate([sums, top, total, jnp.zeros((6, ctx_count * rows), jnp.float32)], 0)
    return pack.reshape(hd + 8, ctx_count, rows).transpose(1, 0, 2)


def merge(packs, hd, heads):
    top = jnp.max(packs[:, hd : hd + 1], 0)
    factor = jnp.exp(packs[:, hd : hd + 1] - top)
    total = jnp.sum(factor * packs[:, hd + 1 : hd + 2], 0)
    out = (jnp.sum(factor * packs[:, :hd], 0) / total).astype(jnp.bfloat16)
    block = out.shape[1] // heads
    return out.reshape(hd, heads, block).transpose(2, 1, 0).reshape(block, heads * hd)


def route_tables(expert_ids, gate_weights, exp_dev):
    block = expert_ids.shape[0]
    both = jnp.concatenate([expert_ids.astype(jnp.float32), gate_weights], 1)
    both = lax.all_gather(both, ("req", "ctx"))
    blocks = both.shape[0]
    ids = both[:, :, :TOP].astype(jnp.int32)
    gates = both[:, :, TOP:]
    first = lax.axis_index("req") * exp_dev
    experts = first + jnp.arange(exp_dev, dtype=jnp.int32)
    hits = ids[:, :, :, None] == experts
    gate_at = jnp.sum(jnp.where(hits, gates[..., None], 0.0), 2)
    hit = jnp.any(hits, 2)
    earlier = jnp.tril(jnp.ones((block, block), jnp.bfloat16), -1)
    rank = jnp.einsum(
        "ij,bje->bie", earlier, hit.astype(jnp.bfloat16), preferred_element_type=jnp.float32
    )
    code = jnp.arange(blocks, dtype=jnp.int32)[:, None, None] * CAP + rank.astype(jnp.int32)
    code = jnp.where(hit, code, -1)
    flat = (blocks * block, exp_dev)
    return code.reshape(flat).T, gate_at.reshape(flat).T


def spread_body(
    queries,
    new_keys,
    new_values,
    cache_keys,
    cache_values,
    cache_lengths,
    residual,
    out_weight,
    norm_gain,
    expert_ids,
    gate_weights,
    w_gate,
    w_up,
    w_down,
):
    ctx_pos, tp_pos, req_pos = (lax.axis_index(a) for a in ("ctx", "tp", "req"))
    ctx_count, req_count = lax.axis_size("ctx"), lax.axis_size("req")
    tok_dev, heads, hd = queries.shape
    block, share = residual.shape
    exp_dev = w_gate.shape[0]
    slots = req_count * ctx_count * CAP
    length = lax.dynamic_index_in_dim(cache_lengths, req_pos, 0, keepdims=False)
    code, gate_at = route_tables(expert_ids, gate_weights, exp_dev)
    swap = [(a * ctx_count + b, b * ctx_count + a) for a in range(ctx_count) for b in range(ctx_count)]
    residual_t = lax.ppermute(residual, ("ctx", "tp"), swap)
    packs = attention_part(queries, new_keys, new_values, cache_keys, cache_values, length)
    packs = lax.all_to_all(packs, "ctx", 0, 0, tiled=True)
    attended = merge(packs, hd, heads)
    attended = lax.all_gather(attended, "ctx", tiled=True)
    part = jnp.dot(attended, out_weight, preferred_element_type=jnp.float32)
    part = part.reshape(-1, block, share)
    part = lax.all_to_all(part, "tp", 0, 0, tiled=True)
    hidden = jnp.sum(part, 0) + residual_t.astype(jnp.float32)
    squares = jnp.sum(hidden * hidden, 1)
    gain = lax.dynamic_slice_in_dim(norm_gain, ctx_pos * share, share, 0)
    scaled = (hidden * gain).astype(jnp.bfloat16)
    squares = lax.psum(squares, "ctx")
    factor = lax.rsqrt(squares / norm_gain.shape[0] + 1e-6)
    factor = lax.all_gather(factor, ("req", "tp"), tiled=True)
    scaled = lax.all_gather(scaled, ("req", "tp"), tiled=True)
    pick = code[:, None, :] == jnp.arange(slots, dtype=jnp.int32)[None, :, None]
    row_factor = jnp.sum(jnp.where(pick, factor, 0.0), -1, keepdims=True)
    row_gate = jnp.sum(jnp.where(pick, gate_at[:, None, :], 0.0), -1, keepdims=True)
    pick = pick.astype(jnp.bfloat16)
    rows = jnp.einsum("est,td->esd", pick, scaled, preferred_element_type=jnp.bfloat16)
    gate = jnp.einsum("esd,edf->esf", rows, w_gate, preferred_element_type=jnp.float32)
    up = jnp.einsum("esd,edf->esf", rows, w_up, preferred_element_type=jnp.float32)
    both = jnp.stack([gate, up], 2).astype(jnp.bfloat16)
    both = both.reshape(ctx_count, exp_dev * slots // ctx_count, 2, -1)
    both = lax.all_to_all(both, "ctx", 0, 0, tiled=True)
    both = both.astype(jnp.float32).sum(0)
    per = exp_dev * slots // ctx_count
    mine = lax.dynamic_slice_in_dim(row_factor.reshape(-1, 1), ctx_pos * per, per, 0)
    inner = (jax.nn.silu(both[:, 0] * mine) * (both[:, 1] * mine)).astype(jnp.bfloat16)
    inner = lax.all_gather(inner, "ctx", tiled=True).reshape(exp_dev, slots, -1)
    down = jnp.einsum("esf,efd->esd", inner, w_down, preferred_element_type=jnp.float32)
    down = (down * row_gate).astype(jnp.bfloat16)
    mixed = jnp.einsum("est,esd->td", pick, down, preferred_element_type=jnp.float32)
    mixed = mixed.astype(jnp.bfloat16).reshape(-1, block, share)
    mixed = lax.all_to_all(mixed, ("req", "tp"), 0, 0, tiled=True)
    out = hidden + jnp.sum(mixed.astype(jnp.float32), 0)
    return lax.ppermute(out.astype(jnp.bfloat16), ("ctx", "tp"), swap)


def body(*args):
    tokens = args[0].shape[0] * lax.axis_size("req")
    slots = args[11].shape[0] * lax.axis_size("req") * lax.axis_size("ctx") * CAP
    if tokens * slots * 2 <= FUSED_BYTES:
        return fused_body(*args)
    return spread_body(*args)


def solution(mesh):
    in_specs = (
        P("req", "tp", None),
        P("req", "tp", None),
        P("req", "tp", None),
        P("req", "ctx", "tp", None),
        P("req", "ctx", "tp", None),
        P(),
        P(("req", "ctx"), "tp"),
        P("tp", "ctx"),
        P(),
        P(("req", "ctx"), None),
        P(("req", "ctx"), None),
        P("req", "ctx", "tp"),
        P("req", "ctx", "tp"),
        P("req", "tp", "ctx"),
    )
    out_specs = P(("req", "ctx"), "tp")
    return jax.shard_map(body, mesh=mesh, in_specs=in_specs, out_specs=out_specs, check_vma=False)
```

```python
import functools
import jax
import jax.numpy as jnp
from jax import lax
from jax.experimental import pallas as pl
from jax.experimental.pallas import tpu as pltpu
from jax.sharding import PartitionSpec as P

TOP = 6
CAP = 8
MASKED = -1e30
F32 = jnp.float32
BF16 = jnp.bfloat16
GROUPS = 4
PIECES = 2
HALVES = 2
ORDER = (
    "U0 P0 U1 W1",
    "P1 W2 P2 A0",
    "W3 P3 P4 A1",
    "A2 A3 A4 P5",
    "P6 P7 S0 S1",
    "S2 S3 D0 D1",
    "S4 D2 D3 D4",
    "A5 A6 A7 S5",
    "S6 D5 S7 D6",
    "D7",
)
FUSED_BYTES = 4 * 1024 * 1024


def dot(a, b, contract, kind=F32):
    return lax.dot_general(a, b, (contract, ((), ())), preferred_element_type=kind)


def layer_kernel(
    dims,
    len_ref,
    ids_ref,
    gw_ref,
    gain_ref,
    res_ref,
    q_hbm,
    ck_hbm,
    cv_hbm,
    nk_hbm,
    nv_hbm,
    ow_hbm,
    wg_hbm,
    wu_hbm,
    wd_hbm,
    out_ref,
    wg,
    wu,
    wd,
    keys,
    vals,
    nvals,
    qa,
    ow,
    rt,
    pk_send,
    pk_recv,
    st_send,
    st_recv,
    turned,
    att,
    part,
    part_recv,
    res_t,
    hidden,
    sq,
    fac,
    frows,
    tab,
    codes,
    tok,
    pick,
    pickg,
    x,
    gu,
    r1,
    s2,
    r2,
    p1,
    p2,
    inner,
    ys,
    acc,
    mix,
    mix_recv,
    tsend,
    trecv,
    w_sem,
    ssem,
    rsem,
    gssem,
    grsem,
    tssem,
    trsem,
    fssem,
    frsem,
):
    reqs, ctxs, tps, block, heads, hd, exp_dev, slots, ff, share = dims
    r, c, t = lax.axis_index("req"), lax.axis_index("ctx"), lax.axis_index("tp")
    blocks = reqs * ctxs
    own_toks = ctxs * block
    rb = ctxs * CAP
    members = exp_dev // GROUPS
    chunk = members * rb
    quarter = chunk // ctxs
    plan = (
        [(0, 0)]
        + [(g, a) for a in range(1, reqs) for g in range(GROUPS)]
        + [(g, 0) for g in range(1, GROUPS)]
    )
    y, k = c // 2, c % 2
    count = [0]

    def remote(src, dst, send, recv, where):
        return pltpu.make_async_remote_copy(
            src_ref=src,
            dst_ref=dst,
            send_sem=send,
            recv_sem=recv,
            device_id={"req": r, "ctx": c, "tp": t} | where,
            device_id_type=pl.DeviceIdType.MESH,
        )

    def rcopy(src, dst, **where):
        i = count[0]
        count[0] = i + 1
        return remote(src, dst, ssem.at[i], rsem.at[i], where)

    def step(me, d, n):
        return lax.rem(me + d, n)

    cache_dev = ck_hbm.shape[0]
    rows = heads * block
    fresh = pl.ds(pl.multiple_of(c * block, block), block)
    loads = [
        pltpu.make_async_copy(src, dst, w_sem.at[i])
        for i, (src, dst) in enumerate(
            [
                (q_hbm, qa.at[:, 0:hd]),
                (ck_hbm, keys.at[0:cache_dev, 0:hd]),
                (nk_hbm.at[fresh], keys.at[cache_dev : cache_dev + block, 0:hd]),
                (cv_hbm, vals),
                (nv_hbm.at[fresh], nvals),
                (ow_hbm, ow),
                (wg_hbm, wg),
                (wu_hbm, wu),
                (wd_hbm, wd),
            ]
        )
    ]
    for load in loads[:6]:
        load.start()

    barrier = pltpu.get_barrier_semaphore()
    peers = [
        {"req": step(r, a, reqs), "ctx": step(c, b, ctxs), "tp": t}
        for a in range(reqs)
        for b in range(ctxs)
        if a or b
    ] + [
        {"req": step(r, a, reqs), "ctx": c, "tp": step(t, d, tps)}
        for a in range(reqs)
        for d in range(1, tps)
    ]
    swap = {"ctx": t, "tp": c}
    across = [{"req": r, "ctx": step(c, d, ctxs), "tp": c} for d in range(1, ctxs)] + [
        {"req": r, "ctx": t, "tp": step(t, d, tps)} for d in range(1, tps)
    ]

    def greet(peer):
        pl.semaphore_signal(barrier, 1, device_id=peer, device_id_type=pl.DeviceIdType.MESH)

    for peer in peers:
        greet(peer)

    @pl.when(c != t)
    def _():
        for peer in across:
            greet(peer)
        pl.semaphore_wait(barrier, len(peers) + len(across))

    @pl.when(c == t)
    def _():
        pl.semaphore_wait(barrier, len(peers))

    pending = []

    me = r * ctxs + c
    res_copy = rcopy(res_ref, res_t, **swap)

    @pl.when(c != t)
    def _():
        res_copy.start()

    @pl.when(c == t)
    def _():
        res_t[...] = res_ref[...]

    length = len_ref[r]
    scale = hd**-0.5
    lean = scale * 1.4426950408889634
    wide = keys.shape[1]
    old_at = lax.broadcasted_iota(jnp.int32, (cache_dev, wide - hd), 0)
    lane_at = lax.broadcasted_iota(jnp.int32, (cache_dev, wide - hd), 1)
    hide = jnp.logical_and(old_at >= length - c * cache_dev, lane_at == 0)
    keys[0:cache_dev, hd:wide] = jnp.where(hide, MASKED, 0.0).astype(BF16)
    qa[:, hd:wide] = jnp.ones((ctxs * rows, wide - hd), BF16)
    new_at = lax.broadcasted_iota(jnp.int32, (block, rows), 0) + c * block
    tok_at = lax.broadcasted_iota(jnp.int32, (block, rows), 1) // heads
    stat_at = lax.broadcasted_iota(jnp.int32, (8, rows), 0)
    for load in loads[:5]:
        load.wait()
    for load in loads[6:]:
        load.start()
    tile = cache_dev // 4
    pk_copies = []
    tab_copies = []
    for d in list(range(1, ctxs)) + [0]:
        b = step(c, d, ctxs)
        at = pl.ds(pl.multiple_of(b * rows, rows), rows)
        scores = [
            dot(keys[i : i + tile, :], qa[at, :], ((1,), (1,))) for i in range(0, cache_dev, tile)
        ]
        new = dot(keys[cache_dev : cache_dev + block, 0:hd], qa[at, 0:hd], ((1,), (1,)))
        scores.append(jnp.where(new_at <= tok_at + b * block, new, MASKED))
        tops = [jnp.max(s, 0, keepdims=True) for s in scores]
        top = jnp.maximum(functools.reduce(jnp.maximum, tops), -1e28)
        total, sums = None, None
        for i, s in enumerate(scores):
            w = jnp.exp2((s - top) * lean)
            v = vals[i * tile : (i + 1) * tile, :] if i * tile < cache_dev else nvals[...]
            part_total = jnp.sum(w, 0, keepdims=True)
            part_sums = dot(v, w.astype(BF16), ((0,), (0,)))
            total = part_total if total is None else total + part_total
            sums = part_sums if sums is None else sums + part_sums
        pk_send[d] = sums.astype(BF16)
        st_send[d] = jnp.where(
            stat_at == 0, top * scale, jnp.where(stat_at == 1, total, 0.0)
        )
        if d:
            for src, dst in ((pk_send, pk_recv), (st_send, st_recv)):
                copy = rcopy(src.at[d], dst.at[d], ctx=b)
                copy.start()
                pk_copies.append(copy)
        if d == 1:
            n_exp = reqs * exp_dev
            ids = jnp.concatenate([ids_ref[...]] * (128 // block), 1)
            gws = jnp.concatenate([gw_ref[...]] * (128 // block), 1)
            half = lax.broadcasted_iota(jnp.int32, ids.shape, 1) // block
            ids = jnp.where(half == lax.rem(me, 128 // block), ids, -1)
            exp_at = lax.broadcasted_iota(jnp.int32, (n_exp, 128), 0)
            hit = jnp.zeros((n_exp, 128), F32)
            gates = jnp.zeros((n_exp, 128), F32)
            for route in range(TOP):
                same = ids[route : route + 1, :] == exp_at
                hit = hit + jnp.where(same, 1.0, 0.0)
                gates = gates + jnp.where(same, gws[route : route + 1, :], 0.0)
            one_at = lax.broadcasted_iota(jnp.int32, (128, 128), 0)
            two_at = lax.broadcasted_iota(jnp.int32, (128, 128), 1)
            upto = jnp.where(one_at <= two_at, 1.0, 0.0).astype(BF16)
            rank = dot(hit.astype(BF16), upto, ((1,), (0,)))
            code = jnp.where(hit > 0.0, rank + (c * CAP).astype(F32), 0.0)
            for a in range(reqs):
                rt[a, 0:exp_dev, :] = code[a * exp_dev : (a + 1) * exp_dev]
                rt[a, exp_dev : 2 * exp_dev, :] = gates[a * exp_dev : (a + 1) * exp_dev]
            for a in range(reqs):
                for b2 in range(ctxs):
                    if a or b2:
                        to = step(r, a, reqs)
                        copy = rcopy(rt.at[to], tab.at[me], req=to, ctx=step(c, b2, ctxs))
                        copy.start()
                        tab_copies.append(copy)
            tab[me] = rt[r]
    for copy in pk_copies:
        copy.wait_recv()
    pending += pk_copies
    packs = [pk_send[0]] + [pk_recv[d] for d in range(1, ctxs)]
    stats = [st_send[0]] + [st_recv[d] for d in range(1, ctxs)]
    tops = [st[0:1, :] for st in stats]
    top = functools.reduce(jnp.maximum, tops)
    total = jnp.zeros((1, rows), F32)
    sums = jnp.zeros((hd, rows), F32)
    for p, st, own in zip(packs, stats, tops):
        factor = jnp.exp(own - top)
        total = total + factor * st[1:2, :]
        sums = sums + factor * p.astype(F32)
    turned[...] = jnp.transpose(sums / total)
    for h in range(heads):
        att[c, :, h * hd : (h + 1) * hd] = turned[pl.ds(h, block, stride=heads), :].astype(BF16)
    att_copies = []
    for d in range(1, ctxs):
        copy = rcopy(att.at[c], att.at[c], ctx=step(c, d, ctxs))
        copy.start()
        att_copies.append(copy)
    for copy in tab_copies:
        copy.wait_recv()
    pending += tab_copies
    for a in range(reqs):
        at = step(r, a, reqs) * ctxs
        for p in range(ctxs // 2):
            codes[a, :, p * 128 : (p + 1) * 128] = tab[at + 2 * p] + tab[at + 2 * p + 1]
    slot_at = lax.broadcasted_iota(jnp.int32, (rb, own_toks), 0).astype(F32) + 1.0

    def make_pick(e, carry):
        at = pl.ds(pl.multiple_of(e * rb, rb), rb)
        for a in range(reqs):
            mine = slot_at == codes[a, pl.ds(e, 1), :]
            gate = codes[a, pl.ds(exp_dev + e, 1), :]
            pick[a, at, :] = jnp.where(mine, 1.0, 0.0).astype(BF16)
            pickg[a, at, :] = jnp.where(mine, gate, 0.0).astype(BF16)
        return carry

    lax.fori_loop(0, exp_dev, make_pick, 0)
    loads[5].wait()
    for copy in att_copies:
        copy.wait_recv()
    pending += att_copies
    width = heads * hd
    full = dot(att[...].reshape(ctxs * block, width), ow[...], ((1,), (0,)))
    half = share // HALVES
    part_copies = []
    for p in range(HALVES):
        part[p] = full[:, p * half : (p + 1) * half].reshape(tps, block, half).astype(BF16)
        for d in range(1, tps):
            to = step(t, d, tps)
            copy = rcopy(part.at[p, to], part_recv.at[p, d], tp=to)
            copy.start()
            part_copies.append(copy)

    @pl.when(c != t)
    def _():
        res_copy.wait_recv()

    lanes = share // 128
    mine = t
    sent = []

    def relay(at, to, i, side, where, cond, p):
        copy = remote(
            tok.at[at, :, p * half : (p + 1) * half],
            tok.at[to, :, p * half : (p + 1) * half],
            tssem.at[i, side, p],
            trsem.at[to, p],
            where,
        )
        sent.append((copy, cond))
        pl.when(cond)(copy.start)

    def landed(at, cond, p):
        view = tok.at[at, :, p * half : (p + 1) * half]
        copy = remote(view, view, tssem.at[0, 0, p], trsem.at[at, p], {"tp": step(t, 1, tps)})
        pl.when(cond)(copy.wait_recv)

    def relay_far(at, i, cond, p):
        for a in range(1, reqs):
            relay(at, (reqs - a) * tps + at, i, 1 + a, {"req": step(r, a, reqs)}, cond, p)

    up_to, down_to = {"tp": jnp.minimum(t + 1, tps - 1)}, {"tp": jnp.maximum(t - 1, 0)}
    for p in range(HALVES):
        sl = slice(p * half, (p + 1) * half)
        hid = part[p, t].astype(F32) + res_t[:, sl].astype(F32)
        for d in range(1, tps):
            part_copies[p * (tps - 1) + d - 1].wait_recv()
            hid = hid + part_recv[p, d].astype(F32)
        hidden[:, sl] = hid
        for q in range(lanes // HALVES):
            q_at = p * (lanes // HALVES) + q
            tok[mine, :, q_at * 128 : (q_at + 1) * 128] = (
                hid[:, q * 128 : (q + 1) * 128] * gain_ref[pl.ds(c * lanes + q_at, 1), :]
            ).astype(BF16)
        relay(mine, mine, 0, 0, up_to, t < tps - 1, p)
        relay(mine, mine, 0, 1, down_to, t > 0, p)
        relay_far(mine, 0, t >= 0, p)
    pending += part_copies
    hid = hidden[...]
    squares = jnp.broadcast_to(jnp.sum(hid * hid, 1, keepdims=True), (block, 128))
    squares = jnp.concatenate([squares] * (128 // block), 0)
    sq[0] = jnp.transpose(squares)[0:8]
    sq_copies = []
    for d in range(1, ctxs):
        copy = rcopy(sq.at[0], sq.at[d], ctx=step(c, d, ctxs))
        copy.start()
        sq_copies.append(copy)
    for hop in range(1, tps):
        for p in range(HALVES):
            for side, from_at, inside, onward, where in (
                (0, t - hop, t >= hop, t < tps - 1, up_to),
                (1, t + hop, t < tps - hop, t > 0, down_to),
            ):
                at = jnp.clip(from_at, 0, tps - 1)
                landed(at, inside, p)
                if hop < tps - 1:
                    relay(at, at, hop, side, where, jnp.logical_and(inside, onward), p)
                relay_far(at, hop + side * (tps - 1), inside, p)
    for copy in sq_copies:
        copy.wait_recv()
    pending += sq_copies
    squares = sq[0]
    for d in range(1, ctxs):
        squares = squares + sq[d]
    fac[mine] = lax.rsqrt(squares / (share * ctxs) + 1e-6)
    for a in range(reqs):
        for d in range(tps):
            if a or d:
                there = (reqs - a) % reqs * tps + t
                copy = remote(
                    fac.at[mine],
                    fac.at[there],
                    fssem.at[a, d],
                    frsem.at[there],
                    {"req": step(r, a, reqs), "tp": step(t, d, tps)},
                )
                copy.start()
                pending.append(copy)
    for load in loads[6:8]:
        load.wait()
    n_q = quarter // rb
    first, second, third, fourth = {}, [], [], []

    def up_stage(*js):
        g = plan[js[0]][0]
        for j in js:
            a = plan[j][1]
            x[a] = dot(
                pick[a, g * chunk : (g + 1) * chunk, :],
                tok[a * tps : (a + 1) * tps].reshape(own_toks, share),
                ((1,), (0,)),
            ).astype(BF16)

        def one(i, carry):
            e = g * members + i
            at = pl.ds(pl.multiple_of((i % n_q) * rb, rb), rb)
            from_at = pl.ds(pl.multiple_of(i * rb, rb), rb)
            xs = jnp.concatenate([x[plan[j][1], from_at, :] for j in js], 0)
            q = i // n_q
            for w, weight in enumerate((wg, wu)):
                res = dot(xs, weight[e], ((1,), (1,))).astype(BF16)
                for m, j in enumerate(js):
                    gu[w, j, q // 2, q % 2, at, :] = res[m * rb : (m + 1) * rb]
            return carry

        lax.fori_loop(0, members, one, 0, unroll=min(4, members))
        for j in js:
            copy = rcopy(gu.at[:, j, :, 1 - k], r1.at[:, j], ctx=y * 2 + 1 - k)
            copy.start()
            first[j] = copy

    def both_stage(g):
        up_stage(*[j for j in range(len(plan)) if plan[j][0] == g])

    whole = ff // 128 * 128

    def pack(ref, j, arrays, cuts):
        at = 0
        for v in arrays:
            for m in range(0, whole, 128):
                ref[j, at : at + quarter, :] = v[:, m : m + 128].astype(BF16)
                at += quarter
        n = quarter // cuts
        ends = jnp.concatenate(
            [v[i * n : (i + 1) * n, whole:ff] for v in arrays for i in range(cuts)], 1
        )
        for m in range(0, ends.shape[1], 128):
            ref[j, at : at + n, :] = ends[:, m : m + 128].astype(BF16)
            at += n

    def unpack(ref, j, count_of, cuts):
        at = 0
        mains = []
        for _ in range(count_of):
            tiles = []
            for _ in range(0, whole, 128):
                tiles.append(ref[j, at : at + quarter, :].astype(F32))
                at += quarter
            mains.append(tiles)
        n, rest = quarter // cuts, ff - whole
        ends = []
        for _ in range(0, count_of * cuts * rest, 128):
            ends.append(ref[j, at : at + n, :].astype(F32))
            at += n
        ends = jnp.concatenate(ends, 1)
        out = []
        for v in range(count_of):
            last = [
                ends[:, i * rest : (i + 1) * rest] for i in range(v * cuts, (v + 1) * cuts)
            ]
            out.append(jnp.concatenate(mains[v] + [jnp.concatenate(last, 0)], 1))
        return out

    def pair_stage(j):
        first[j].wait_recv()
        both = gu[:, j, 1 - y, k].astype(F32) + r1[:, j, 1 - y].astype(F32)
        pack(s2, j, [both[0], both[1]], 2)
        copy = rcopy(s2.at[j], r2.at[j], ctx=(1 - y) * 2 + k)
        copy.start()
        second.append(copy)

    def factor_rows(a):
        for d in range(tps):
            if a or d:
                at = a * tps + step(t, d, tps)
                remote(
                    fac.at[at],
                    fac.at[at],
                    fssem.at[0, 1],
                    frsem.at[at],
                    {"tp": step(t, 1, tps)},
                ).wait_recv()
        low_lane = lax.broadcasted_iota(jnp.int32, (8, 128), 1) < block
        row_at = lax.broadcasted_iota(jnp.int32, (8, 128), 0)
        for p in range(tps // 2):
            f = jnp.where(low_lane, fac[a * tps + 2 * p], fac[a * tps + 2 * p + 1])
            hi = f.astype(BF16).astype(F32)
            mid = (f - hi).astype(BF16).astype(F32)
            low = f - hi - mid
            f = jnp.where(row_at == 0, hi, jnp.where(row_at == 1, mid, low))
            frows[a, :, p * 128 : (p + 1) * 128] = jnp.where(row_at < 3, f, 0.0).astype(BF16)

    def act_stage(j):
        second[j].wait_recv()
        both = gu[:, j, y, k].astype(F32) + r1[:, j, y].astype(F32)
        other = unpack(r2, j, 2, 2)
        g, a = plan[j]
        mine = pick[a, pl.ds(pl.multiple_of(g * chunk + c * quarter, quarter), quarter), :]
        row = jnp.sum(dot(mine, frows[a], ((1,), (1,))), 1, keepdims=True)
        gate = (both[0] + other[0]) * row
        act = gate * jax.nn.sigmoid(gate) * ((both[1] + other[1]) * row)
        pack(p1, j, [act], 4)
        copy = rcopy(p1.at[j], p2.at[j], ctx=(1 - y) * 2 + k)
        copy.start()
        third.append(copy)
        inner[j, y, k] = act.astype(BF16)

    def share_stage(j):
        third[j].wait_recv()
        inner[j, 1 - y, k] = unpack(p2, j, 1, 4)[0].astype(BF16)
        copy = rcopy(inner.at[j, :, k], inner.at[j, :, k], ctx=y * 2 + 1 - k)
        copy.start()
        fourth.append(copy)

    per = tps * block
    mix_copies = []

    def down_stage(j):
        fourth[j].wait_recv()
        g, a = plan[j]

        def one(i, carry):
            e = g * members + i
            q = i // n_q
            at = pl.ds(pl.multiple_of((i % n_q) * rb, rb), rb)
            down = dot(inner[j, q // 2, q % 2, at, :], wd[e], ((1,), (0,)))
            ys[pl.ds(pl.multiple_of(i * rb, rb), rb), :] = down.astype(BF16)
            return carry

        lax.fori_loop(0, members, one, 0, unroll=min(4, members))
        term = dot(pickg[a, g * chunk : (g + 1) * chunk, :], ys[...], ((0,), (0,)))
        if g == 0:
            acc[a] = term
        else:
            acc[a] += term
        if a and g == GROUPS - 1:
            mix[a] = acc[a].astype(BF16)
            copy = rcopy(mix.at[a], mix_recv.at[a], req=step(r, a, reqs))
            copy.start()
            mix_copies.append(copy)

    stages = {"U": up_stage, "W": both_stage, "P": pair_stage, "A": act_stage, "S": share_stage, "D": down_stage}
    for line in ORDER:
        for item in line.split():
            j = int(item[1:])
            if item[0] == "U" and plan[j][1] and plan[j][0] == 0:
                for d in range(tps):
                    for p in range(HALVES):
                        landed(plan[j][1] * tps + d, t >= 0, p)
            if item[0] == "A" and plan[j][0] == 0:
                factor_rows(plan[j][1])
            if item == "D0":
                loads[8].wait()
            stages[item[0]](j)
    pending += list(first.values()) + second + third + fourth

    cols = share // PIECES
    pending += mix_copies
    for copy in mix_copies:
        copy.wait_recv()
    for piece in range(PIECES):
        sl = slice(piece * cols, (piece + 1) * cols)
        mixed = acc[0, :, sl]
        own = pl.ds(pl.multiple_of(t * block, block), block)
        with_hidden = acc[0, own, sl] + hidden[:, sl]
        for a in range(1, reqs):
            mixed = mixed + mix_recv[a, :, sl].astype(F32)
            with_hidden = with_hidden + mix_recv[a, own, sl].astype(F32)
        tsend[piece] = mixed.reshape(tps, block, cols).astype(BF16)
        tsend[piece, t] = with_hidden.astype(BF16)
        for d in range(1, ctxs):
            to = step(c, d, ctxs)
            copy = remote(
                tsend.at[piece, to],
                trecv.at[piece, t],
                gssem.at[piece, d],
                grsem.at[piece, t],
                {"ctx": to, "tp": c},
            )
            copy.start()
            pending.append(copy)

        @pl.when(c != t)
        def _():
            remote(
                tsend.at[piece, c],
                trecv.at[piece, t],
                gssem.at[piece, 0],
                grsem.at[piece, t],
                {"tp": c},
            ).start()

        @pl.when(c == t)
        def _():
            trecv[piece, t] = tsend[piece, c]

    for piece in range(PIECES):
        sl = slice(piece * cols, (piece + 1) * cols)

        def arrival(d):
            at = step(t, d, tps)
            return remote(
                tsend.at[piece, 0],
                trecv.at[piece, at],
                gssem.at[piece, 0],
                grsem.at[piece, at],
                {"ctx": step(c, 1, ctxs)},
            )

        @pl.when(c != t)
        def _():
            arrival(0).wait_recv()

        total = trecv[piece, t].astype(F32)
        for d in range(1, tps):
            arrival(d).wait_recv()
            total = total + trecv[piece, step(t, d, tps)].astype(F32)
        out_ref[:, sl] = total.astype(BF16)

    @pl.when(c != t)
    def _():
        res_copy.wait_send()
        for piece in range(PIECES):
            remote(
                tsend.at[piece, c],
                trecv.at[piece, t],
                gssem.at[piece, 0],
                grsem.at[piece, t],
                {"tp": c},
            ).wait_send()

    for copy, cond in sent:
        pl.when(cond)(copy.wait_send)
    for copy in pending:
        copy.wait_send()


def fused_body(
    queries,
    new_keys,
    new_values,
    cache_keys,
    cache_values,
    cache_lengths,
    residual,
    out_weight,
    norm_gain,
    expert_ids,
    gate_weights,
    w_gate,
    w_up,
    w_down,
):
    reqs, ctxs, tps = (lax.axis_size(a) for a in ("req", "ctx", "tp"))
    tok_dev, heads, hd = queries.shape
    block, share = residual.shape
    exp_dev, _, ff = w_gate.shape
    cache_dev = cache_keys.shape[1]
    blocks = reqs * ctxs
    slots = blocks * CAP
    chunks = GROUPS * reqs
    own_toks = ctxs * block
    chunk = exp_dev // GROUPS * ctxs * CAP
    quarter = chunk // ctxs
    rows = heads * block
    per, cols = tps * block, share // PIECES
    pair_rows = 2 * quarter * ff // 128
    dims = (reqs, ctxs, tps, block, heads, hd, exp_dev, slots, ff, share)
    n_rem = (
        (blocks - 1)
        + 2
        + 3 * (ctxs - 1)
        + HALVES * (tps - 1)
        + (ctxs - 1)
        + 4 * chunks
        + (reqs - 1)
    )
    vmem = pl.BlockSpec(memory_space=pltpu.VMEM)
    anywhere = pl.BlockSpec(memory_space=pl.ANY)
    scratch = [
        ((exp_dev, ff, share), BF16),
        ((exp_dev, ff, share), BF16),
        ((exp_dev, ff, share), BF16),
        ((cache_dev + block, hd + 128), BF16),
        ((cache_dev, hd), BF16),
        ((block, hd), BF16),
        ((ctxs * rows, hd + 128), BF16),
        ((heads * hd, share), BF16),
        ((reqs, 2 * exp_dev, 128), F32),
        ((ctxs, hd, rows), BF16),
        ((ctxs, hd, rows), BF16),
        ((ctxs, 8, rows), F32),
        ((ctxs, 8, rows), F32),
        ((rows, hd), F32),
        ((ctxs, block, heads * hd), BF16),
        ((HALVES, tps, block, share // HALVES), BF16),
        ((HALVES, tps, block, share // HALVES), BF16),
        ((block, share), BF16),
        ((block, share), F32),
        ((ctxs, 8, 128), F32),
        ((reqs * tps, 8, 128), F32),
        ((reqs, 8, own_toks), BF16),
        ((blocks, 2 * exp_dev, 128), F32),
        ((reqs, 2 * exp_dev, own_toks), F32),
        ((reqs * tps, block, share), BF16),
        ((reqs, exp_dev * ctxs * CAP, own_toks), BF16),
        ((reqs, exp_dev * ctxs * CAP, own_toks), BF16),
        ((reqs, chunk, share), BF16),
        ((2, chunks, 2, 2, quarter, ff), BF16),
        ((2, chunks, 2, quarter, ff), BF16),
        ((chunks, pair_rows, 128), BF16),
        ((chunks, pair_rows, 128), BF16),
        ((chunks, pair_rows // 2, 128), BF16),
        ((chunks, pair_rows // 2, 128), BF16),
        ((chunks, 2, 2, quarter, ff), BF16),
        ((chunk, share), BF16),
        ((reqs, own_toks, share), F32),
        ((reqs, per, share), BF16),
        ((reqs, per, share), BF16),
        ((PIECES, tps, block, cols), BF16),
        ((PIECES, tps, block, cols), BF16),
    ]
    return pl.pallas_call(
        functools.partial(layer_kernel, dims),
        out_shape=jax.ShapeDtypeStruct((block, share), BF16),
        in_specs=[pl.BlockSpec(memory_space=pltpu.SMEM)] + [vmem] * 4 + [anywhere] * 9,
        out_specs=vmem,
        scratch_shapes=[pltpu.VMEM(*s) for s in scratch]
        + [
            pltpu.SemaphoreType.DMA((9,)),
            pltpu.SemaphoreType.DMA((n_rem,)),
            pltpu.SemaphoreType.DMA((n_rem,)),
            pltpu.SemaphoreType.DMA((PIECES, ctxs)),
            pltpu.SemaphoreType.DMA((PIECES, tps)),
            pltpu.SemaphoreType.DMA((2 * tps - 1, reqs + 1, HALVES)),
            pltpu.SemaphoreType.DMA((reqs * tps, HALVES)),
            pltpu.SemaphoreType.DMA((reqs, tps)),
            pltpu.SemaphoreType.DMA((reqs * tps,)),
        ],
        compiler_params=pltpu.CompilerParams(
            collective_id=0, has_side_effects=True, vmem_limit_bytes=63 * 1024 * 1024
        ),
    )(
        cache_lengths,
        expert_ids.T,
        gate_weights.T,
        norm_gain.reshape(-1, 128),
        residual,
        queries.reshape(tok_dev * heads, hd),
        cache_keys[0, :, 0, :],
        cache_values[0, :, 0, :],
        new_keys[:, 0, :],
        new_values[:, 0, :],
        out_weight,
        jnp.swapaxes(w_gate, 1, 2),
        jnp.swapaxes(w_up, 1, 2),
        w_down,
    )


def attention_part(queries, new_keys, new_values, cache_keys, cache_values, length):
    ctx_pos, ctx_count = lax.axis_index("ctx"), lax.axis_size("ctx")
    tok_dev, heads, hd = queries.shape
    cache_dev = cache_keys.shape[1]
    block = tok_dev // ctx_count
    rows = heads * block
    q = queries.reshape(ctx_count, block, heads, hd).transpose(0, 2, 1, 3)
    q = q.reshape(ctx_count * rows, hd)
    keys = jnp.concatenate([cache_keys[0, :, 0, :], new_keys[:, 0, :]], 0)
    values = jnp.concatenate([cache_values[0, :, 0, :], new_values[:, 0, :]], 0)
    scores = jnp.dot(keys, q.T, preferred_element_type=jnp.float32) * (hd**-0.5)
    key_at = jnp.arange(cache_dev + tok_dev, dtype=jnp.int32)[:, None]
    row_at = jnp.arange(ctx_count * rows, dtype=jnp.int32)[None, :]
    token = (row_at // rows) * block + row_at % block
    valid = jnp.where(
        key_at < cache_dev,
        ctx_pos * cache_dev + key_at < length,
        jnp.logical_and(ctx_pos == ctx_count - 1, key_at - cache_dev <= token),
    )
    scores = jnp.where(valid, scores, MASKED)
    top = jnp.max(scores, 0, keepdims=True)
    weights = jnp.where(valid, jnp.exp(scores - top), 0.0)
    total = jnp.sum(weights, 0, keepdims=True)
    sums = lax.dot_general(
        values,
        weights.astype(jnp.bfloat16),
        (((0,), (0,)), ((), ())),
        preferred_element_type=jnp.float32,
    )
    pack = jnp.concatenate([sums, top, total, jnp.zeros((6, ctx_count * rows), jnp.float32)], 0)
    return pack.reshape(hd + 8, ctx_count, rows).transpose(1, 0, 2)


def merge(packs, hd, heads):
    top = jnp.max(packs[:, hd : hd + 1], 0)
    factor = jnp.exp(packs[:, hd : hd + 1] - top)
    total = jnp.sum(factor * packs[:, hd + 1 : hd + 2], 0)
    out = (jnp.sum(factor * packs[:, :hd], 0) / total).astype(jnp.bfloat16)
    block = out.shape[1] // heads
    return out.reshape(hd, heads, block).transpose(2, 1, 0).reshape(block, heads * hd)


def route_tables(expert_ids, gate_weights, exp_dev):
    block = expert_ids.shape[0]
    both = jnp.concatenate([expert_ids.astype(jnp.float32), gate_weights], 1)
    both = lax.all_gather(both, ("req", "ctx"))
    blocks = both.shape[0]
    ids = both[:, :, :TOP].astype(jnp.int32)
    gates = both[:, :, TOP:]
    first = lax.axis_index("req") * exp_dev
    experts = first + jnp.arange(exp_dev, dtype=jnp.int32)
    hits = ids[:, :, :, None] == experts
    gate_at = jnp.sum(jnp.where(hits, gates[..., None], 0.0), 2)
    hit = jnp.any(hits, 2)
    earlier = jnp.tril(jnp.ones((block, block), jnp.bfloat16), -1)
    rank = jnp.einsum(
        "ij,bje->bie", earlier, hit.astype(jnp.bfloat16), preferred_element_type=jnp.float32
    )
    code = jnp.arange(blocks, dtype=jnp.int32)[:, None, None] * CAP + rank.astype(jnp.int32)
    code = jnp.where(hit, code, -1)
    flat = (blocks * block, exp_dev)
    return code.reshape(flat).T, gate_at.reshape(flat).T


def spread_body(
    queries,
    new_keys,
    new_values,
    cache_keys,
    cache_values,
    cache_lengths,
    residual,
    out_weight,
    norm_gain,
    expert_ids,
    gate_weights,
    w_gate,
    w_up,
    w_down,
):
    ctx_pos, tp_pos, req_pos = (lax.axis_index(a) for a in ("ctx", "tp", "req"))
    ctx_count, req_count = lax.axis_size("ctx"), lax.axis_size("req")
    tok_dev, heads, hd = queries.shape
    block, share = residual.shape
    exp_dev = w_gate.shape[0]
    slots = req_count * ctx_count * CAP
    length = lax.dynamic_index_in_dim(cache_lengths, req_pos, 0, keepdims=False)
    code, gate_at = route_tables(expert_ids, gate_weights, exp_dev)
    swap = [(a * ctx_count + b, b * ctx_count + a) for a in range(ctx_count) for b in range(ctx_count)]
    residual_t = lax.ppermute(residual, ("ctx", "tp"), swap)
    packs = attention_part(queries, new_keys, new_values, cache_keys, cache_values, length)
    packs = lax.all_to_all(packs, "ctx", 0, 0, tiled=True)
    attended = merge(packs, hd, heads)
    attended = lax.all_gather(attended, "ctx", tiled=True)
    part = jnp.dot(attended, out_weight, preferred_element_type=jnp.float32)
    part = part.reshape(-1, block, share)
    part = lax.all_to_all(part, "tp", 0, 0, tiled=True)
    hidden = jnp.sum(part, 0) + residual_t.astype(jnp.float32)
    squares = jnp.sum(hidden * hidden, 1)
    gain = lax.dynamic_slice_in_dim(norm_gain, ctx_pos * share, share, 0)
    scaled = (hidden * gain).astype(jnp.bfloat16)
    squares = lax.psum(squares, "ctx")
    factor = lax.rsqrt(squares / norm_gain.shape[0] + 1e-6)
    factor = lax.all_gather(factor, ("req", "tp"), tiled=True)
    scaled = lax.all_gather(scaled, ("req", "tp"), tiled=True)
    pick = code[:, None, :] == jnp.arange(slots, dtype=jnp.int32)[None, :, None]
    row_factor = jnp.sum(jnp.where(pick, factor, 0.0), -1, keepdims=True)
    row_gate = jnp.sum(jnp.where(pick, gate_at[:, None, :], 0.0), -1, keepdims=True)
    pick = pick.astype(jnp.bfloat16)
    rows = jnp.einsum("est,td->esd", pick, scaled, preferred_element_type=jnp.bfloat16)
    gate = jnp.einsum("esd,edf->esf", rows, w_gate, preferred_element_type=jnp.float32)
    up = jnp.einsum("esd,edf->esf", rows, w_up, preferred_element_type=jnp.float32)
    both = jnp.stack([gate, up], 2).astype(jnp.bfloat16)
    both = both.reshape(ctx_count, exp_dev * slots // ctx_count, 2, -1)
    both = lax.all_to_all(both, "ctx", 0, 0, tiled=True)
    both = both.astype(jnp.float32).sum(0)
    per = exp_dev * slots // ctx_count
    mine = lax.dynamic_slice_in_dim(row_factor.reshape(-1, 1), ctx_pos * per, per, 0)
    inner = (jax.nn.silu(both[:, 0] * mine) * (both[:, 1] * mine)).astype(jnp.bfloat16)
    inner = lax.all_gather(inner, "ctx", tiled=True).reshape(exp_dev, slots, -1)
    down = jnp.einsum("esf,efd->esd", inner, w_down, preferred_element_type=jnp.float32)
    down = (down * row_gate).astype(jnp.bfloat16)
    mixed = jnp.einsum("est,esd->td", pick, down, preferred_element_type=jnp.float32)
    mixed = mixed.astype(jnp.bfloat16).reshape(-1, block, share)
    mixed = lax.all_to_all(mixed, ("req", "tp"), 0, 0, tiled=True)
    out = hidden + jnp.sum(mixed.astype(jnp.float32), 0)
    return lax.ppermute(out.astype(jnp.bfloat16), ("ctx", "tp"), swap)


def body(*args):
    tokens = args[0].shape[0] * lax.axis_size("req")
    slots = args[11].shape[0] * lax.axis_size("req") * lax.axis_size("ctx") * CAP
    if tokens * slots * 2 <= FUSED_BYTES:
        return fused_body(*args)
    return spread_body(*args)


def solution(mesh):
    in_specs = (
        P("req", "tp", None),
        P("req", "tp", None),
        P("req", "tp", None),
        P("req", "ctx", "tp", None),
        P("req", "ctx", "tp", None),
        P(),
        P(("req", "ctx"), "tp"),
        P("tp", "ctx"),
        P(),
        P(("req", "ctx"), None),
        P(("req", "ctx"), None),
        P("req", "ctx", "tp"),
        P("req", "ctx", "tp"),
        P("req", "tp", "ctx"),
    )
    out_specs = P(("req", "ctx"), "tp")
    return jax.shard_map(body, mesh=mesh, in_specs=in_specs, out_specs=out_specs, check_vma=False)
```

```python
import functools
import jax
import jax.numpy as jnp
from jax import lax
from jax.experimental import pallas as pl
from jax.experimental.pallas import tpu as pltpu
from jax.sharding import PartitionSpec as P

TOP = 6
CAP = 8
MASKED = -1e30
F32 = jnp.float32
BF16 = jnp.bfloat16
GROUPS = 4
PIECES = 2
HALVES = 2
ORDER = (
    "U0 P0 U1 W1",
    "P1 W2 P2 A0",
    "W3 P3 P4 A1",
    "A2 A3 A4 P5",
    "P6 P7 S0 S1",
    "S2 S3 D0 D1",
    "S4 D2 D3 D4",
    "A5 A6 A7 S5",
    "S6 D5 S7 D6",
    "D7",
)
FUSED_BYTES = 4 * 1024 * 1024


def dot(a, b, contract, kind=F32):
    return lax.dot_general(a, b, (contract, ((), ())), preferred_element_type=kind)


def layer_kernel(
    dims,
    len_ref,
    ids_ref,
    gw_ref,
    gain_ref,
    res_ref,
    q_hbm,
    ck_hbm,
    cv_hbm,
    nk_hbm,
    nv_hbm,
    ow_hbm,
    wg_hbm,
    wu_hbm,
    wd_hbm,
    out_ref,
    wg,
    wu,
    wd,
    keys,
    vals,
    nvals,
    qa,
    ow,
    rt,
    pk_send,
    pk_recv,
    st_send,
    st_recv,
    turned,
    att,
    part,
    part_recv,
    res_t,
    hidden,
    sq,
    fac,
    frows,
    tab,
    codes,
    tok,
    pick,
    pickg,
    x,
    gu,
    r1,
    s2,
    r2,
    p1,
    p2,
    inner,
    ys,
    acc,
    mix,
    mix_recv,
    tsend,
    trecv,
    w_sem,
    ssem,
    rsem,
    gssem,
    grsem,
    tssem,
    trsem,
    fssem,
    frsem,
):
    reqs, ctxs, tps, block, heads, hd, exp_dev, slots, ff, share = dims
    r, c, t = lax.axis_index("req"), lax.axis_index("ctx"), lax.axis_index("tp")
    blocks = reqs * ctxs
    own_toks = ctxs * block
    rb = ctxs * CAP
    members = exp_dev // GROUPS
    chunk = members * rb
    quarter = chunk // ctxs
    plan = (
        [(0, 0)]
        + [(g, a) for a in range(1, reqs) for g in range(GROUPS)]
        + [(g, 0) for g in range(1, GROUPS)]
    )
    y, k = c // 2, c % 2
    count = [0]

    def remote(src, dst, send, recv, where):
        return pltpu.make_async_remote_copy(
            src_ref=src,
            dst_ref=dst,
            send_sem=send,
            recv_sem=recv,
            device_id={"req": r, "ctx": c, "tp": t} | where,
            device_id_type=pl.DeviceIdType.MESH,
        )

    def rcopy(src, dst, **where):
        i = count[0]
        count[0] = i + 1
        return remote(src, dst, ssem.at[i], rsem.at[i], where)

    def step(me, d, n):
        return lax.rem(me + d, n)

    cache_dev = ck_hbm.shape[0]
    rows = heads * block
    fresh = pl.ds(pl.multiple_of(c * block, block), block)
    loads = [
        pltpu.make_async_copy(src, dst, w_sem.at[i])
        for i, (src, dst) in enumerate(
            [
                (q_hbm, qa.at[:, 0:hd]),
                (ck_hbm, keys.at[0:cache_dev, 0:hd]),
                (nk_hbm.at[fresh], keys.at[cache_dev : cache_dev + block, 0:hd]),
                (cv_hbm, vals),
                (nv_hbm.at[fresh], nvals),
                (ow_hbm, ow),
                (wg_hbm, wg),
                (wu_hbm, wu),
                (wd_hbm, wd),
            ]
        )
    ]
    for load in loads[:6]:
        load.start()

    barrier = pltpu.get_barrier_semaphore()
    peers = [
        {"req": step(r, a, reqs), "ctx": step(c, b, ctxs), "tp": t}
        for a in range(reqs)
        for b in range(ctxs)
        if a or b
    ] + [
        {"req": step(r, a, reqs), "ctx": c, "tp": step(t, d, tps)}
        for a in range(reqs)
        for d in range(1, tps)
    ]
    swap = {"ctx": t, "tp": c}
    across = [{"req": r, "ctx": step(c, d, ctxs), "tp": c} for d in range(1, ctxs)] + [
        {"req": r, "ctx": t, "tp": step(t, d, tps)} for d in range(1, tps)
    ]

    def greet(peer):
        pl.semaphore_signal(barrier, 1, device_id=peer, device_id_type=pl.DeviceIdType.MESH)

    for peer in peers:
        greet(peer)

    @pl.when(c != t)
    def _():
        for peer in across:
            greet(peer)
        pl.semaphore_wait(barrier, len(peers) + len(across))

    @pl.when(c == t)
    def _():
        pl.semaphore_wait(barrier, len(peers))

    pending = []

    me = r * ctxs + c
    res_copy = rcopy(res_ref, res_t, **swap)

    @pl.when(c != t)
    def _():
        res_copy.start()

    @pl.when(c == t)
    def _():
        res_t[...] = res_ref[...]

    length = len_ref[r]
    scale = hd**-0.5
    lean = scale * 1.4426950408889634
    wide = keys.shape[1]
    old_at = lax.broadcasted_iota(jnp.int32, (cache_dev, wide - hd), 0)
    lane_at = lax.broadcasted_iota(jnp.int32, (cache_dev, wide - hd), 1)
    hide = jnp.logical_and(old_at >= length - c * cache_dev, lane_at == 0)
    keys[0:cache_dev, hd:wide] = jnp.where(hide, MASKED, 0.0).astype(BF16)
    qa[:, hd:wide] = jnp.ones((ctxs * rows, wide - hd), BF16)
    new_at = lax.broadcasted_iota(jnp.int32, (block, rows), 0) + c * block
    tok_at = lax.broadcasted_iota(jnp.int32, (block, rows), 1) // heads
    stat_at = lax.broadcasted_iota(jnp.int32, (8, rows), 0)
    for load in loads[:5]:
        load.wait()
    for load in loads[6:]:
        load.start()
    tile = cache_dev // 4
    pk_copies = []
    tab_copies = []
    for d in list(range(1, ctxs)) + [0]:
        b = step(c, d, ctxs)
        at = pl.ds(pl.multiple_of(b * rows, rows), rows)
        scores = [
            dot(keys[i : i + tile, :], qa[at, :], ((1,), (1,))) for i in range(0, cache_dev, tile)
        ]
        new = dot(keys[cache_dev : cache_dev + block, 0:hd], qa[at, 0:hd], ((1,), (1,)))
        scores.append(jnp.where(new_at <= tok_at + b * block, new, MASKED))
        tops = [jnp.max(s, 0, keepdims=True) for s in scores]
        top = jnp.maximum(functools.reduce(jnp.maximum, tops), -1e28)
        total, sums = None, None
        for i, s in enumerate(scores):
            w = jnp.exp2((s - top) * lean)
            v = vals[i * tile : (i + 1) * tile, :] if i * tile < cache_dev else nvals[...]
            part_total = jnp.sum(w, 0, keepdims=True)
            part_sums = dot(v, w.astype(BF16), ((0,), (0,)))
            total = part_total if total is None else total + part_total
            sums = part_sums if sums is None else sums + part_sums
        pk_send[d] = sums.astype(BF16)
        st_send[d] = jnp.where(
            stat_at == 0, top * scale, jnp.where(stat_at == 1, total, 0.0)
        )
        if d:
            for src, dst in ((pk_send, pk_recv), (st_send, st_recv)):
                copy = rcopy(src.at[d], dst.at[d], ctx=b)
                copy.start()
                pk_copies.append(copy)
        if d == 1:
            n_exp = reqs * exp_dev
            ids = jnp.concatenate([ids_ref[...]] * (128 // block), 1)
            gws = jnp.concatenate([gw_ref[...]] * (128 // block), 1)
            half = lax.broadcasted_iota(jnp.int32, ids.shape, 1) // block
            ids = jnp.where(half == lax.rem(me, 128 // block), ids, -1)
            exp_at = lax.broadcasted_iota(jnp.int32, (n_exp, 128), 0)
            hit = jnp.zeros((n_exp, 128), F32)
            gates = jnp.zeros((n_exp, 128), F32)
            for route in range(TOP):
                same = ids[route : route + 1, :] == exp_at
                hit = hit + jnp.where(same, 1.0, 0.0)
                gates = gates + jnp.where(same, gws[route : route + 1, :], 0.0)
            one_at = lax.broadcasted_iota(jnp.int32, (128, 128), 0)
            two_at = lax.broadcasted_iota(jnp.int32, (128, 128), 1)
            upto = jnp.where(one_at <= two_at, 1.0, 0.0).astype(BF16)
            rank = dot(hit.astype(BF16), upto, ((1,), (0,)))
            code = jnp.where(hit > 0.0, rank + (c * CAP).astype(F32), 0.0)
            for a in range(reqs):
                rt[a, 0:exp_dev, :] = code[a * exp_dev : (a + 1) * exp_dev].astype(BF16)
                rt[a, exp_dev : 2 * exp_dev, :] = gates[a * exp_dev : (a + 1) * exp_dev].astype(BF16)
            for a in range(reqs):
                for b2 in range(ctxs):
                    if a or b2:
                        to = step(r, a, reqs)
                        copy = rcopy(rt.at[to], tab.at[me], req=to, ctx=step(c, b2, ctxs))
                        copy.start()
                        tab_copies.append(copy)
            tab[me] = rt[r]
    for copy in pk_copies:
        copy.wait_recv()
    pending += pk_copies
    packs = [pk_send[0]] + [pk_recv[d] for d in range(1, ctxs)]
    stats = [st_send[0]] + [st_recv[d] for d in range(1, ctxs)]
    tops = [st[0:1, :] for st in stats]
    top = functools.reduce(jnp.maximum, tops)
    total = jnp.zeros((1, rows), F32)
    sums = jnp.zeros((hd, rows), F32)
    for p, st, own in zip(packs, stats, tops):
        factor = jnp.exp(own - top)
        total = total + factor * st[1:2, :]
        sums = sums + factor * p.astype(F32)
    turned[...] = jnp.transpose(sums / total)
    for h in range(heads):
        att[c, :, h * hd : (h + 1) * hd] = turned[pl.ds(h, block, stride=heads), :].astype(BF16)
    att_copies = []
    for d in range(1, ctxs):
        copy = rcopy(att.at[c], att.at[c], ctx=step(c, d, ctxs))
        copy.start()
        att_copies.append(copy)
    for copy in tab_copies:
        copy.wait_recv()
    pending += tab_copies
    for a in range(reqs):
        at = step(r, a, reqs) * ctxs
        for p in range(ctxs // 2):
            even, odd = tab[at + 2 * p].astype(F32), tab[at + 2 * p + 1].astype(F32)
            codes[a, :, p * 128 : (p + 1) * 128] = even + odd
    slot_at = lax.broadcasted_iota(jnp.int32, (rb, own_toks), 0).astype(F32) + 1.0

    def make_pick(e, carry):
        at = pl.ds(pl.multiple_of(e * rb, rb), rb)
        for a in range(reqs):
            mine = slot_at == codes[a, pl.ds(e, 1), :]
            gate = codes[a, pl.ds(exp_dev + e, 1), :]
            pick[a, at, :] = jnp.where(mine, 1.0, 0.0).astype(BF16)
            pickg[a, at, :] = jnp.where(mine, gate, 0.0).astype(BF16)
        return carry

    lax.fori_loop(0, exp_dev, make_pick, 0)
    loads[5].wait()
    for copy in att_copies:
        copy.wait_recv()
    pending += att_copies
    width = heads * hd
    full = dot(att[...].reshape(ctxs * block, width), ow[...], ((1,), (0,)))
    half = share // HALVES
    part_copies = []
    for p in range(HALVES):
        part[p] = full[:, p * half : (p + 1) * half].reshape(tps, block, half).astype(BF16)
        for d in range(1, tps):
            to = step(t, d, tps)
            copy = rcopy(part.at[p, to], part_recv.at[p, d], tp=to)
            copy.start()
            part_copies.append(copy)

    @pl.when(c != t)
    def _():
        res_copy.wait_recv()

    lanes = share // 128
    mine = t
    sent = []

    def relay(at, to, i, side, where, cond, p):
        copy = remote(
            tok.at[at, :, p * half : (p + 1) * half],
            tok.at[to, :, p * half : (p + 1) * half],
            tssem.at[i, side, p],
            trsem.at[to, p],
            where,
        )
        sent.append((copy, cond))
        pl.when(cond)(copy.start)

    def landed(at, cond, p):
        view = tok.at[at, :, p * half : (p + 1) * half]
        copy = remote(view, view, tssem.at[0, 0, p], trsem.at[at, p], {"tp": step(t, 1, tps)})
        pl.when(cond)(copy.wait_recv)

    def relay_far(at, i, cond, p):
        for a in range(1, reqs):
            relay(at, (reqs - a) * tps + at, i, 1 + a, {"req": step(r, a, reqs)}, cond, p)

    up_to, down_to = {"tp": jnp.minimum(t + 1, tps - 1)}, {"tp": jnp.maximum(t - 1, 0)}
    for p in range(HALVES):
        sl = slice(p * half, (p + 1) * half)
        hid = part[p, t].astype(F32) + res_t[:, sl].astype(F32)
        for d in range(1, tps):
            part_copies[p * (tps - 1) + d - 1].wait_recv()
            hid = hid + part_recv[p, d].astype(F32)
        hidden[:, sl] = hid
        for q in range(lanes // HALVES):
            q_at = p * (lanes // HALVES) + q
            tok[mine, :, q_at * 128 : (q_at + 1) * 128] = (
                hid[:, q * 128 : (q + 1) * 128] * gain_ref[pl.ds(c * lanes + q_at, 1), :]
            ).astype(BF16)
        relay(mine, mine, 0, 0, up_to, t < tps - 1, p)
        relay(mine, mine, 0, 1, down_to, t > 0, p)
        relay_far(mine, 0, t >= 0, p)
    pending += part_copies
    hid = hidden[...]
    squares = jnp.broadcast_to(jnp.sum(hid * hid, 1, keepdims=True), (block, 128))
    squares = jnp.concatenate([squares] * (128 // block), 0)
    sq[0] = jnp.transpose(squares)[0:8]
    sq_copies = []
    for d in range(1, ctxs):
        copy = rcopy(sq.at[0], sq.at[d], ctx=step(c, d, ctxs))
        copy.start()
        sq_copies.append(copy)
    for hop in range(1, tps):
        for p in range(HALVES):
            for side, from_at, inside, onward, where in (
                (0, t - hop, t >= hop, t < tps - 1, up_to),
                (1, t + hop, t < tps - hop, t > 0, down_to),
            ):
                at = jnp.clip(from_at, 0, tps - 1)
                landed(at, inside, p)
                if hop < tps - 1:
                    relay(at, at, hop, side, where, jnp.logical_and(inside, onward), p)
                relay_far(at, hop + side * (tps - 1), inside, p)
    for copy in sq_copies:
        copy.wait_recv()
    pending += sq_copies
    squares = sq[0]
    for d in range(1, ctxs):
        squares = squares + sq[d]
    fac[mine] = lax.rsqrt(squares / (share * ctxs) + 1e-6)
    for a in range(reqs):
        for d in range(tps):
            if a or d:
                there = (reqs - a) % reqs * tps + t
                copy = remote(
                    fac.at[mine],
                    fac.at[there],
                    fssem.at[a, d],
                    frsem.at[there],
                    {"req": step(r, a, reqs), "tp": step(t, d, tps)},
                )
                copy.start()
                pending.append(copy)
    for load in loads[6:8]:
        load.wait()
    n_q = quarter // rb
    first, second, third, fourth = {}, [], [], []

    def up_stage(*js):
        g = plan[js[0]][0]
        for j in js:
            a = plan[j][1]
            x[a] = dot(
                pick[a, g * chunk : (g + 1) * chunk, :],
                tok[a * tps : (a + 1) * tps].reshape(own_toks, share),
                ((1,), (0,)),
            ).astype(BF16)

        def one(i, carry):
            e = g * members + i
            at = pl.ds(pl.multiple_of((i % n_q) * rb, rb), rb)
            from_at = pl.ds(pl.multiple_of(i * rb, rb), rb)
            xs = jnp.concatenate([x[plan[j][1], from_at, :] for j in js], 0)
            q = i // n_q
            for w, weight in enumerate((wg, wu)):
                res = dot(xs, weight[e], ((1,), (1,))).astype(BF16)
                for m, j in enumerate(js):
                    gu[w, j, q // 2, q % 2, at, :] = res[m * rb : (m + 1) * rb]
            return carry

        lax.fori_loop(0, members, one, 0, unroll=min(4, members))
        for j in js:
            copy = rcopy(gu.at[:, j, :, 1 - k], r1.at[:, j], ctx=y * 2 + 1 - k)
            copy.start()
            first[j] = copy

    def both_stage(g):
        up_stage(*[j for j in range(len(plan)) if plan[j][0] == g])

    whole = ff // 128 * 128

    def pack(ref, j, arrays, cuts):
        at = 0
        for v in arrays:
            for m in range(0, whole, 128):
                ref[j, at : at + quarter, :] = v[:, m : m + 128].astype(BF16)
                at += quarter
        n = quarter // cuts
        ends = jnp.concatenate(
            [v[i * n : (i + 1) * n, whole:ff] for v in arrays for i in range(cuts)], 1
        )
        for m in range(0, ends.shape[1], 128):
            ref[j, at : at + n, :] = ends[:, m : m + 128].astype(BF16)
            at += n

    def unpack(ref, j, count_of, cuts):
        at = 0
        mains = []
        for _ in range(count_of):
            tiles = []
            for _ in range(0, whole, 128):
                tiles.append(ref[j, at : at + quarter, :].astype(F32))
                at += quarter
            mains.append(tiles)
        n, rest = quarter // cuts, ff - whole
        ends = []
        for _ in range(0, count_of * cuts * rest, 128):
            ends.append(ref[j, at : at + n, :].astype(F32))
            at += n
        ends = jnp.concatenate(ends, 1)
        out = []
        for v in range(count_of):
            last = [
                ends[:, i * rest : (i + 1) * rest] for i in range(v * cuts, (v + 1) * cuts)
            ]
            out.append(jnp.concatenate(mains[v] + [jnp.concatenate(last, 0)], 1))
        return out

    def pair_stage(j):
        first[j].wait_recv()
        both = gu[:, j, 1 - y, k].astype(F32) + r1[:, j, 1 - y].astype(F32)
        pack(s2, j, [both[0], both[1]], 2)
        copy = rcopy(s2.at[j], r2.at[j], ctx=(1 - y) * 2 + k)
        copy.start()
        second.append(copy)

    def factor_rows(a):
        for d in range(tps):
            if a or d:
                at = a * tps + step(t, d, tps)
                remote(
                    fac.at[at],
                    fac.at[at],
                    fssem.at[0, 1],
                    frsem.at[at],
                    {"tp": step(t, 1, tps)},
                ).wait_recv()
        low_lane = lax.broadcasted_iota(jnp.int32, (8, 128), 1) < block
        row_at = lax.broadcasted_iota(jnp.int32, (8, 128), 0)
        for p in range(tps // 2):
            f = jnp.where(low_lane, fac[a * tps + 2 * p], fac[a * tps + 2 * p + 1])
            hi = f.astype(BF16).astype(F32)
            mid = (f - hi).astype(BF16).astype(F32)
            low = f - hi - mid
            f = jnp.where(row_at == 0, hi, jnp.where(row_at == 1, mid, low))
            frows[a, :, p * 128 : (p + 1) * 128] = jnp.where(row_at < 3, f, 0.0).astype(BF16)

    def act_stage(j):
        second[j].wait_recv()
        both = gu[:, j, y, k].astype(F32) + r1[:, j, y].astype(F32)
        other = unpack(r2, j, 2, 2)
        g, a = plan[j]
        mine = pick[a, pl.ds(pl.multiple_of(g * chunk + c * quarter, quarter), quarter), :]
        row = jnp.sum(dot(mine, frows[a], ((1,), (1,))), 1, keepdims=True)
        gate = (both[0] + other[0]) * row
        act = gate * jax.nn.sigmoid(gate) * ((both[1] + other[1]) * row)
        pack(p1, j, [act], 4)
        copy = rcopy(p1.at[j], p2.at[j], ctx=(1 - y) * 2 + k)
        copy.start()
        third.append(copy)
        inner[j, y, k] = act.astype(BF16)

    def share_stage(j):
        third[j].wait_recv()
        inner[j, 1 - y, k] = unpack(p2, j, 1, 4)[0].astype(BF16)
        copy = rcopy(inner.at[j, :, k], inner.at[j, :, k], ctx=y * 2 + 1 - k)
        copy.start()
        fourth.append(copy)

    per = tps * block
    mix_copies = []

    def down_stage(j):
        fourth[j].wait_recv()
        g, a = plan[j]

        def one(i, carry):
            e = g * members + i
            q = i // n_q
            at = pl.ds(pl.multiple_of((i % n_q) * rb, rb), rb)
            down = dot(inner[j, q // 2, q % 2, at, :], wd[e], ((1,), (0,)))
            ys[pl.ds(pl.multiple_of(i * rb, rb), rb), :] = down.astype(BF16)
            return carry

        lax.fori_loop(0, members, one, 0, unroll=min(4, members))
        term = dot(pickg[a, g * chunk : (g + 1) * chunk, :], ys[...], ((0,), (0,)))
        if g == 0:
            acc[a] = term
        else:
            acc[a] += term
        if a and g == GROUPS - 1:
            mix[a] = acc[a].astype(BF16)
            copy = rcopy(mix.at[a], mix_recv.at[a], req=step(r, a, reqs))
            copy.start()
            mix_copies.append(copy)

    stages = {"U": up_stage, "W": both_stage, "P": pair_stage, "A": act_stage, "S": share_stage, "D": down_stage}
    for line in ORDER:
        for item in line.split():
            j = int(item[1:])
            if item[0] == "U" and plan[j][1] and plan[j][0] == 0:
                for d in range(tps):
                    for p in range(HALVES):
                        landed(plan[j][1] * tps + d, t >= 0, p)
            if item[0] == "A" and plan[j][0] == 0:
                factor_rows(plan[j][1])
            if item == "D0":
                loads[8].wait()
            stages[item[0]](j)
    pending += list(first.values()) + second + third + fourth

    cols = share // PIECES
    pending += mix_copies
    for copy in mix_copies:
        copy.wait_recv()
    for piece in range(PIECES):
        sl = slice(piece * cols, (piece + 1) * cols)
        mixed = acc[0, :, sl]
        own = pl.ds(pl.multiple_of(t * block, block), block)
        with_hidden = acc[0, own, sl] + hidden[:, sl]
        for a in range(1, reqs):
            mixed = mixed + mix_recv[a, :, sl].astype(F32)
            with_hidden = with_hidden + mix_recv[a, own, sl].astype(F32)
        tsend[piece] = mixed.reshape(tps, block, cols).astype(BF16)
        tsend[piece, t] = with_hidden.astype(BF16)
        for d in range(1, ctxs):
            to = step(c, d, ctxs)
            copy = remote(
                tsend.at[piece, to],
                trecv.at[piece, t],
                gssem.at[piece, d],
                grsem.at[piece, t],
                {"ctx": to, "tp": c},
            )
            copy.start()
            pending.append(copy)

        @pl.when(c != t)
        def _():
            remote(
                tsend.at[piece, c],
                trecv.at[piece, t],
                gssem.at[piece, 0],
                grsem.at[piece, t],
                {"tp": c},
            ).start()

        @pl.when(c == t)
        def _():
            trecv[piece, t] = tsend[piece, c]

    for piece in range(PIECES):
        sl = slice(piece * cols, (piece + 1) * cols)

        def arrival(d):
            at = step(t, d, tps)
            return remote(
                tsend.at[piece, 0],
                trecv.at[piece, at],
                gssem.at[piece, 0],
                grsem.at[piece, at],
                {"ctx": step(c, 1, ctxs)},
            )

        @pl.when(c != t)
        def _():
            arrival(0).wait_recv()

        total = trecv[piece, t].astype(F32)
        for d in range(1, tps):
            arrival(d).wait_recv()
            total = total + trecv[piece, step(t, d, tps)].astype(F32)
        out_ref[:, sl] = total.astype(BF16)

    @pl.when(c != t)
    def _():
        res_copy.wait_send()
        for piece in range(PIECES):
            remote(
                tsend.at[piece, c],
                trecv.at[piece, t],
                gssem.at[piece, 0],
                grsem.at[piece, t],
                {"tp": c},
            ).wait_send()

    for copy, cond in sent:
        pl.when(cond)(copy.wait_send)
    for copy in pending:
        copy.wait_send()


def fused_body(
    queries,
    new_keys,
    new_values,
    cache_keys,
    cache_values,
    cache_lengths,
    residual,
    out_weight,
    norm_gain,
    expert_ids,
    gate_weights,
    w_gate,
    w_up,
    w_down,
):
    reqs, ctxs, tps = (lax.axis_size(a) for a in ("req", "ctx", "tp"))
    tok_dev, heads, hd = queries.shape
    block, share = residual.shape
    exp_dev, _, ff = w_gate.shape
    cache_dev = cache_keys.shape[1]
    blocks = reqs * ctxs
    slots = blocks * CAP
    chunks = GROUPS * reqs
    own_toks = ctxs * block
    chunk = exp_dev // GROUPS * ctxs * CAP
    quarter = chunk // ctxs
    rows = heads * block
    per, cols = tps * block, share // PIECES
    pair_rows = 2 * quarter * ff // 128
    dims = (reqs, ctxs, tps, block, heads, hd, exp_dev, slots, ff, share)
    n_rem = (
        (blocks - 1)
        + 2
        + 3 * (ctxs - 1)
        + HALVES * (tps - 1)
        + (ctxs - 1)
        + 4 * chunks
        + (reqs - 1)
    )
    vmem = pl.BlockSpec(memory_space=pltpu.VMEM)
    anywhere = pl.BlockSpec(memory_space=pl.ANY)
    scratch = [
        ((exp_dev, ff, share), BF16),
        ((exp_dev, ff, share), BF16),
        ((exp_dev, ff, share), BF16),
        ((cache_dev + block, hd + 128), BF16),
        ((cache_dev, hd), BF16),
        ((block, hd), BF16),
        ((ctxs * rows, hd + 128), BF16),
        ((heads * hd, share), BF16),
        ((reqs, 2 * exp_dev, 128), BF16),
        ((ctxs, hd, rows), BF16),
        ((ctxs, hd, rows), BF16),
        ((ctxs, 8, rows), F32),
        ((ctxs, 8, rows), F32),
        ((rows, hd), F32),
        ((ctxs, block, heads * hd), BF16),
        ((HALVES, tps, block, share // HALVES), BF16),
        ((HALVES, tps, block, share // HALVES), BF16),
        ((block, share), BF16),
        ((block, share), F32),
        ((ctxs, 8, 128), F32),
        ((reqs * tps, 8, 128), F32),
        ((reqs, 8, own_toks), BF16),
        ((blocks, 2 * exp_dev, 128), BF16),
        ((reqs, 2 * exp_dev, own_toks), F32),
        ((reqs * tps, block, share), BF16),
        ((reqs, exp_dev * ctxs * CAP, own_toks), BF16),
        ((reqs, exp_dev * ctxs * CAP, own_toks), BF16),
        ((reqs, chunk, share), BF16),
        ((2, chunks, 2, 2, quarter, ff), BF16),
        ((2, chunks, 2, quarter, ff), BF16),
        ((chunks, pair_rows, 128), BF16),
        ((chunks, pair_rows, 128), BF16),
        ((chunks, pair_rows // 2, 128), BF16),
        ((chunks, pair_rows // 2, 128), BF16),
        ((chunks, 2, 2, quarter, ff), BF16),
        ((chunk, share), BF16),
        ((reqs, own_toks, share), F32),
        ((reqs, per, share), BF16),
        ((reqs, per, share), BF16),
        ((PIECES, tps, block, cols), BF16),
        ((PIECES, tps, block, cols), BF16),
    ]
    return pl.pallas_call(
        functools.partial(layer_kernel, dims),
        out_shape=jax.ShapeDtypeStruct((block, share), BF16),
        in_specs=[pl.BlockSpec(memory_space=pltpu.SMEM)] + [vmem] * 4 + [anywhere] * 9,
        out_specs=vmem,
        scratch_shapes=[pltpu.VMEM(*s) for s in scratch]
        + [
            pltpu.SemaphoreType.DMA((9,)),
            pltpu.SemaphoreType.DMA((n_rem,)),
            pltpu.SemaphoreType.DMA((n_rem,)),
            pltpu.SemaphoreType.DMA((PIECES, ctxs)),
            pltpu.SemaphoreType.DMA((PIECES, tps)),
            pltpu.SemaphoreType.DMA((2 * tps - 1, reqs + 1, HALVES)),
            pltpu.SemaphoreType.DMA((reqs * tps, HALVES)),
            pltpu.SemaphoreType.DMA((reqs, tps)),
            pltpu.SemaphoreType.DMA((reqs * tps,)),
        ],
        compiler_params=pltpu.CompilerParams(
            collective_id=0, has_side_effects=True, vmem_limit_bytes=63 * 1024 * 1024
        ),
    )(
        cache_lengths,
        expert_ids.T,
        gate_weights.T,
        norm_gain.reshape(-1, 128),
        residual,
        queries.reshape(tok_dev * heads, hd),
        cache_keys[0, :, 0, :],
        cache_values[0, :, 0, :],
        new_keys[:, 0, :],
        new_values[:, 0, :],
        out_weight,
        jnp.swapaxes(w_gate, 1, 2),
        jnp.swapaxes(w_up, 1, 2),
        w_down,
    )


def attention_part(queries, new_keys, new_values, cache_keys, cache_values, length):
    ctx_pos, ctx_count = lax.axis_index("ctx"), lax.axis_size("ctx")
    tok_dev, heads, hd = queries.shape
    cache_dev = cache_keys.shape[1]
    block = tok_dev // ctx_count
    rows = heads * block
    q = queries.reshape(ctx_count, block, heads, hd).transpose(0, 2, 1, 3)
    q = q.reshape(ctx_count * rows, hd)
    keys = jnp.concatenate([cache_keys[0, :, 0, :], new_keys[:, 0, :]], 0)
    values = jnp.concatenate([cache_values[0, :, 0, :], new_values[:, 0, :]], 0)
    scores = jnp.dot(keys, q.T, preferred_element_type=jnp.float32) * (hd**-0.5)
    key_at = jnp.arange(cache_dev + tok_dev, dtype=jnp.int32)[:, None]
    row_at = jnp.arange(ctx_count * rows, dtype=jnp.int32)[None, :]
    token = (row_at // rows) * block + row_at % block
    valid = jnp.where(
        key_at < cache_dev,
        ctx_pos * cache_dev + key_at < length,
        jnp.logical_and(ctx_pos == ctx_count - 1, key_at - cache_dev <= token),
    )
    scores = jnp.where(valid, scores, MASKED)
    top = jnp.max(scores, 0, keepdims=True)
    weights = jnp.where(valid, jnp.exp(scores - top), 0.0)
    total = jnp.sum(weights, 0, keepdims=True)
    sums = lax.dot_general(
        values,
        weights.astype(jnp.bfloat16),
        (((0,), (0,)), ((), ())),
        preferred_element_type=jnp.float32,
    )
    pack = jnp.concatenate([sums, top, total, jnp.zeros((6, ctx_count * rows), jnp.float32)], 0)
    return pack.reshape(hd + 8, ctx_count, rows).transpose(1, 0, 2)


def merge(packs, hd, heads):
    top = jnp.max(packs[:, hd : hd + 1], 0)
    factor = jnp.exp(packs[:, hd : hd + 1] - top)
    total = jnp.sum(factor * packs[:, hd + 1 : hd + 2], 0)
    out = (jnp.sum(factor * packs[:, :hd], 0) / total).astype(jnp.bfloat16)
    block = out.shape[1] // heads
    return out.reshape(hd, heads, block).transpose(2, 1, 0).reshape(block, heads * hd)


def route_tables(expert_ids, gate_weights, exp_dev):
    block = expert_ids.shape[0]
    both = jnp.concatenate([expert_ids.astype(jnp.float32), gate_weights], 1)
    both = lax.all_gather(both, ("req", "ctx"))
    blocks = both.shape[0]
    ids = both[:, :, :TOP].astype(jnp.int32)
    gates = both[:, :, TOP:]
    first = lax.axis_index("req") * exp_dev
    experts = first + jnp.arange(exp_dev, dtype=jnp.int32)
    hits = ids[:, :, :, None] == experts
    gate_at = jnp.sum(jnp.where(hits, gates[..., None], 0.0), 2)
    hit = jnp.any(hits, 2)
    earlier = jnp.tril(jnp.ones((block, block), jnp.bfloat16), -1)
    rank = jnp.einsum(
        "ij,bje->bie", earlier, hit.astype(jnp.bfloat16), preferred_element_type=jnp.float32
    )
    code = jnp.arange(blocks, dtype=jnp.int32)[:, None, None] * CAP + rank.astype(jnp.int32)
    code = jnp.where(hit, code, -1)
    flat = (blocks * block, exp_dev)
    return code.reshape(flat).T, gate_at.reshape(flat).T


def spread_body(
    queries,
    new_keys,
    new_values,
    cache_keys,
    cache_values,
    cache_lengths,
    residual,
    out_weight,
    norm_gain,
    expert_ids,
    gate_weights,
    w_gate,
    w_up,
    w_down,
):
    ctx_pos, tp_pos, req_pos = (lax.axis_index(a) for a in ("ctx", "tp", "req"))
    ctx_count, req_count = lax.axis_size("ctx"), lax.axis_size("req")
    tok_dev, heads, hd = queries.shape
    block, share = residual.shape
    exp_dev = w_gate.shape[0]
    slots = req_count * ctx_count * CAP
    length = lax.dynamic_index_in_dim(cache_lengths, req_pos, 0, keepdims=False)
    code, gate_at = route_tables(expert_ids, gate_weights, exp_dev)
    swap = [(a * ctx_count + b, b * ctx_count + a) for a in range(ctx_count) for b in range(ctx_count)]
    residual_t = lax.ppermute(residual, ("ctx", "tp"), swap)
    packs = attention_part(queries, new_keys, new_values, cache_keys, cache_values, length)
    packs = lax.all_to_all(packs, "ctx", 0, 0, tiled=True)
    attended = merge(packs, hd, heads)
    attended = lax.all_gather(attended, "ctx", tiled=True)
    part = jnp.dot(attended, out_weight, preferred_element_type=jnp.float32)
    part = part.reshape(-1, block, share)
    part = lax.all_to_all(part, "tp", 0, 0, tiled=True)
    hidden = jnp.sum(part, 0) + residual_t.astype(jnp.float32)
    squares = jnp.sum(hidden * hidden, 1)
    gain = lax.dynamic_slice_in_dim(norm_gain, ctx_pos * share, share, 0)
    scaled = (hidden * gain).astype(jnp.bfloat16)
    squares = lax.psum(squares, "ctx")
    factor = lax.rsqrt(squares / norm_gain.shape[0] + 1e-6)
    factor = lax.all_gather(factor, ("req", "tp"), tiled=True)
    scaled = lax.all_gather(scaled, ("req", "tp"), tiled=True)
    pick = code[:, None, :] == jnp.arange(slots, dtype=jnp.int32)[None, :, None]
    row_factor = jnp.sum(jnp.where(pick, factor, 0.0), -1, keepdims=True)
    row_gate = jnp.sum(jnp.where(pick, gate_at[:, None, :], 0.0), -1, keepdims=True)
    pick = pick.astype(jnp.bfloat16)
    rows = jnp.einsum("est,td->esd", pick, scaled, preferred_element_type=jnp.bfloat16)
    gate = jnp.einsum("esd,edf->esf", rows, w_gate, preferred_element_type=jnp.float32)
    up = jnp.einsum("esd,edf->esf", rows, w_up, preferred_element_type=jnp.float32)
    both = jnp.stack([gate, up], 2).astype(jnp.bfloat16)
    both = both.reshape(ctx_count, exp_dev * slots // ctx_count, 2, -1)
    both = lax.all_to_all(both, "ctx", 0, 0, tiled=True)
    both = both.astype(jnp.float32).sum(0)
    per = exp_dev * slots // ctx_count
    mine = lax.dynamic_slice_in_dim(row_factor.reshape(-1, 1), ctx_pos * per, per, 0)
    inner = (jax.nn.silu(both[:, 0] * mine) * (both[:, 1] * mine)).astype(jnp.bfloat16)
    inner = lax.all_gather(inner, "ctx", tiled=True).reshape(exp_dev, slots, -1)
    down = jnp.einsum("esf,efd->esd", inner, w_down, preferred_element_type=jnp.float32)
    down = (down * row_gate).astype(jnp.bfloat16)
    mixed = jnp.einsum("est,esd->td", pick, down, preferred_element_type=jnp.float32)
    mixed = mixed.astype(jnp.bfloat16).reshape(-1, block, share)
    mixed = lax.all_to_all(mixed, ("req", "tp"), 0, 0, tiled=True)
    out = hidden + jnp.sum(mixed.astype(jnp.float32), 0)
    return lax.ppermute(out.astype(jnp.bfloat16), ("ctx", "tp"), swap)


def body(*args):
    tokens = args[0].shape[0] * lax.axis_size("req")
    slots = args[11].shape[0] * lax.axis_size("req") * lax.axis_size("ctx") * CAP
    if tokens * slots * 2 <= FUSED_BYTES:
        return fused_body(*args)
    return spread_body(*args)


def solution(mesh):
    in_specs = (
        P("req", "tp", None),
        P("req", "tp", None),
        P("req", "tp", None),
        P("req", "ctx", "tp", None),
        P("req", "ctx", "tp", None),
        P(),
        P(("req", "ctx"), "tp"),
        P("tp", "ctx"),
        P(),
        P(("req", "ctx"), None),
        P(("req", "ctx"), None),
        P("req", "ctx", "tp"),
        P("req", "ctx", "tp"),
        P("req", "tp", "ctx"),
    )
    out_specs = P(("req", "ctx"), "tp")
    return jax.shard_map(body, mesh=mesh, in_specs=in_specs, out_specs=out_specs, check_vma=False)
```
